32 devices in a mesh: az: 16 (over z, x, core), el: 2 (over y).
Axes of the slice: x: 2, y: 2, z: 4, core: 2. Of those that a mesh axis runs over, the one named last changes fastest.
Arguments:
- raw_sweeps: bfloat16 [4, 1, 24, 96, 256], P('el', None, None, 'az'), may hold values from -6 to 6
- sweep_ids: int32 [4], P('el'), may hold values from 0 to 3, each once
- elevation_embed: float32 [4, 128], replicated, may hold values from -3 to 3
- input_proj: bfloat16 [24, 128], replicated, may hold values from -0.875 to 0.875
- first_kernel: bfloat16 [3, 3, 128, 128], replicated, may hold values from -0.1875 to 0.1875
- second_kernel: bfloat16 [3, 3, 128, 128], replicated, may hold values from -0.1875 to 0.1875
- join_weight: bfloat16 [2, 128, 128], P('el'), may hold values from -0.375 to 0.375
- head_weight: bfloat16 [12, 128], replicated, may hold values from -0.5 to 0.5
- cotangent: bfloat16 [1, 12, 96, 256], P(None, None, 'az'), may hold values from -6 to 6
Outputs:
- prediction: float32 [1, 12, 96, 256], P(None, None, 'az')
- join_grad: float32 [2, 128, 128], P('el')
- first_kernel_gradient: float32 [3, 3, 128, 128], replicated
- second_kernel_gradient: float32 [3, 3, 128, 128], replicated
- input_grad: float32 [24, 128], replicated
- embed_grad: float32 [4, 128], replicated
The draws below stay inside these ranges and needn't reach their ends.
Inputs may be any that keep to these rules, and one draw needn't show every extreme that they name: `sweep_ids`: each sweep fills exactly one slot.
All inputs are finite; a program needn't handle non-finite values.
Results may differ from the reference program's by a relative error of at most 0.023.
Values may be sent and summed in bfloat16 or wider, within the bound.
A program may use at most 64 MiB of HBM per device.

```python
import jax
import jax.numpy as jnp
from jax import lax

CHANNELS = 128
LEADS = 12
INPUTS = 24
GATES = 256
FIRST_DILATION = 1
SECOND_DILATION = 2
SLOTS = 2
SAMPLES = 1
RAYS = 96
GROUPS = 2
SWEEPS = 4


def levels(rng, extent, pieces, least, largest):
    level, own = 1.0, jax.random.fold_in(rng, 6)
    for dim, blocks in pieces:
        steps = jnp.exp(jax.random.uniform(jax.random.fold_in(own, dim), (blocks,), jnp.float32, least / len(pieces), largest / len(pieces)))
        level = level * jnp.repeat(steps, extent[dim] // blocks).reshape([-1 if axis == dim else 1 for axis in range(len(extent))])
    return level


def normal_values(rng, shape, spread, limit, cuts=(), kind=jnp.bfloat16):
    array = spread * jax.random.normal(rng, shape, jnp.float32)
    if cuts:
        array = array * levels(rng, shape, cuts, -0.22, 0.18)
    return jnp.clip(array, -limit, limit).astype(kind)


def setup_inputs(seed: int = 0) -> dict:
    splits = jax.random.split(jax.random.key(seed), 10)
    raw_sweeps = normal_values(splits[0], (SWEEPS, SAMPLES, INPUTS, RAYS, GATES), 1.0, 6.0, ((0, 2), (3, 16)))
    sweep_ids = jax.random.permutation(splits[1], SWEEPS).astype(jnp.int32)
    elevation_embed = normal_values(splits[2], (SWEEPS, CHANNELS), 0.5, 3.0, (), jnp.float32)
    input_proj = normal_values(splits[3], (INPUTS, CHANNELS), (SLOTS * INPUTS) ** -0.5, 0.875)
    first_kernel = normal_values(splits[4], (3, 3, CHANNELS, CHANNELS), (9 * CHANNELS) ** -0.5, 0.1875)
    second_kernel = normal_values(splits[5], (3, 3, CHANNELS, CHANNELS), (9 * CHANNELS) ** -0.5, 0.1875)
    join_weight = normal_values(splits[6], (GROUPS, CHANNELS, CHANNELS), (GROUPS * CHANNELS) ** -0.5, 0.375, ((0, 2),))
    head_weight = normal_values(splits[7], (LEADS, CHANNELS), CHANNELS ** -0.5, 0.5)
    cotangent = normal_values(splits[8], (SAMPLES, LEADS, RAYS, GATES), 1.0, 6.0, ((2, 16),))
    return dict(raw_sweeps=raw_sweeps, sweep_ids=sweep_ids, elevation_embed=elevation_embed, input_proj=input_proj, first_kernel=first_kernel, second_kernel=second_kernel, join_weight=join_weight, head_weight=head_weight, cotangent=cotangent)


precise = lax.Precision.HIGHEST


def silu_slope(values):
    logistic = jax.nn.sigmoid(values)
    return logistic * (1.0 + values * (1.0 - logistic))


def azimuth_wrap_padding(source, dilate):
    rolled = jnp.concatenate([source[..., -dilate:, :], source, source[..., :dilate, :]], axis=-2)
    pad_spec = [(0, 0)] * (source.ndim - 1) + [(dilate, dilate)]
    return jnp.pad(rolled, pad_spec)


def convolve_layer(padded, kernel, dilate):
    return lax.conv_general_dilated(padded.astype(jnp.float32), kernel.astype(jnp.float32), (1, 1), "VALID",
                                    rhs_dilation=(dilate, dilate), dimension_numbers=("NCHW", "HWIO", "NCHW"),
                                    precision=precise)


def reversed_kernel(kernel):
    return jnp.flip(kernel, (0, 1)).transpose(0, 1, 3, 2)


def kernel_gradient_of(padded, upstream, dilate):
    ray_count = upstream.shape[2]
    gate_count = upstream.shape[3]
    upper = upstream.astype(jnp.float32)
    tap_rows = []
    for tap_row in range(3):
        tap_line = []
        for tap_column in range(3):
            window = padded[:, :, tap_row * dilate:tap_row * dilate + ray_count,
                            tap_column * dilate:tap_column * dilate + gate_count]
            tap_line.append(jnp.einsum("niar,noar->io", window.astype(jnp.float32), upper, precision=precise))
        tap_rows.append(jnp.stack(tap_line))
    return jnp.stack(tap_rows)


def reference(raw_sweeps, sweep_ids, elevation_embed, input_proj, first_kernel, second_kernel, join_weight, head_weight, cotangent):
    brain_float_half = jnp.bfloat16
    grouped = raw_sweeps.reshape((GROUPS, SLOTS) + raw_sweeps.shape[1:])
    onehot = (sweep_ids[:, None] == jnp.arange(SWEEPS, dtype=jnp.int32)[None, :]).astype(jnp.float32)
    bias_rows = jnp.dot(onehot, elevation_embed, precision=precise)
    group_bias = bias_rows.reshape(GROUPS, SLOTS, CHANNELS).sum(axis=1)
    input_state = jnp.einsum("gjbiar,ic->gbcar", grouped.astype(jnp.float32), input_proj.astype(jnp.float32), precision=precise)
    input_state = (input_state + group_bias[:, None, :, None, None]).astype(brain_float_half)
    input_state = input_state.reshape(GROUPS * SAMPLES, CHANNELS, RAYS, GATES)
    input_activation = jax.nn.silu(input_state.astype(jnp.float32)).astype(brain_float_half)
    padded_input = azimuth_wrap_padding(input_activation, FIRST_DILATION)
    hidden_state = (input_state.astype(jnp.float32) + convolve_layer(padded_input, first_kernel, FIRST_DILATION)).astype(brain_float_half)
    hidden_activation = jax.nn.silu(hidden_state.astype(jnp.float32)).astype(brain_float_half)
    padded_hidden = azimuth_wrap_padding(hidden_activation, SECOND_DILATION)
    final_state = (hidden_state.astype(jnp.float32) + convolve_layer(padded_hidden, second_kernel, SECOND_DILATION)).astype(brain_float_half)
    state_group = final_state.reshape(GROUPS, SAMPLES, CHANNELS, RAYS, GATES).astype(jnp.float32)
    joined = jnp.einsum("gbiar,gio->boar", state_group, join_weight.astype(jnp.float32), precision=precise).astype(brain_float_half)
    prediction = jnp.einsum("lc,bcar->blar", head_weight.astype(jnp.float32), joined.astype(jnp.float32), precision=precise)
    joined_back = jnp.einsum("lc,blar->bcar", head_weight.astype(jnp.float32), cotangent.astype(jnp.float32), precision=precise).astype(brain_float_half)
    grad_scale = 1.0 / (GROUPS * SAMPLES * RAYS * GATES) ** 0.5
    join_grad = jnp.einsum("gbiar,boar->gio", state_group, joined_back.astype(jnp.float32), precision=precise)
    grad_two = jnp.einsum("gio,boar->gbiar", join_weight.astype(jnp.float32), joined_back.astype(jnp.float32), precision=precise)
    grad_two = grad_two.reshape(GROUPS * SAMPLES, CHANNELS, RAYS, GATES)
    final_upstream_gradient = grad_two.astype(brain_float_half)
    second_kernel_gradient = kernel_gradient_of(padded_hidden, final_upstream_gradient, SECOND_DILATION)
    second_backward_pass = convolve_layer(azimuth_wrap_padding(final_upstream_gradient, SECOND_DILATION), reversed_kernel(second_kernel), SECOND_DILATION)
    grad_one = grad_two + second_backward_pass * silu_slope(hidden_state.astype(jnp.float32))
    hidden_upstream_gradient = grad_one.astype(brain_float_half)
    first_kernel_gradient = kernel_gradient_of(padded_input, hidden_upstream_gradient, FIRST_DILATION)
    first_backward_pass = convolve_layer(azimuth_wrap_padding(hidden_upstream_gradient, FIRST_DILATION), reversed_kernel(first_kernel), FIRST_DILATION)
    grad_zero = (grad_one + first_backward_pass * silu_slope(input_state.astype(jnp.float32))).astype(brain_float_half)
    grad_zero = grad_zero.reshape(GROUPS, SAMPLES, CHANNELS, RAYS, GATES).astype(jnp.float32)
    input_grad = jnp.einsum("gjbiar,gbcar->ic", grouped.astype(jnp.float32), grad_zero, precision=precise)
    column_sum = grad_zero.sum(axis=(1, 3, 4))
    slot_terms = jnp.repeat(column_sum, SLOTS, axis=0)
    embed_grad = jnp.dot(onehot.T, slot_terms, precision=precise)
    return (prediction, join_grad * grad_scale, first_kernel_gradient * grad_scale, second_kernel_gradient * grad_scale,
            input_grad * grad_scale, embed_grad * grad_scale)
```

```python
import functools
import math

import jax
import jax.numpy as jnp
from jax import lax
from jax.experimental import pallas as pl
from jax.experimental.pallas import tpu as pltpu
from jax.sharding import PartitionSpec as P

C = 128
D1 = 1
D2 = 2
HALO = D1 + D2
BF = jnp.bfloat16
F32 = jnp.float32
MESH = pl.DeviceIdType.MESH
NN = (((1,), (0,)), ((), ()))
NT = (((1,), (1,)), ((), ()))
TN = (((0,), (0,)), ((), ()))


def dot(a, b, dims):
    return lax.dot_general(a, b, dims, preferred_element_type=F32)


def up8(n):
    return -(-n // 8) * 8


def logistic(v):
    return 1.0 / (1.0 + jnp.exp(-v))


def slope(v):
    s = logistic(v)
    return s * (1.0 + v * (1.0 - s))


def layout(sweeps, naz):
    rows = 2 * 9 * C + 24 + up8(sweeps)
    share = up8(-(-rows // naz))
    own = C // naz
    chunk = -(-(share + own) // 16) * 16
    share = chunk - own
    return share, own, chunk


def pieces(start, count, share, chunk):
    out = []
    done = 0
    while done < count:
        k, off = divmod(start + done, share)
        size = min(count - done, share - off)
        out.append((done, k * chunk + off, size))
        done += size
    return out


def fill_taps(ref, value, dilate, gates):
    n = value.shape[1]
    gate = lax.broadcasted_iota(jnp.int32, value.shape, 1) % gates
    low = jnp.where(gate >= dilate, pltpu.roll(value, dilate, 1), 0.0)
    high = jnp.where(gate < gates - dilate, pltpu.roll(value, n - dilate, 1), 0.0)
    ref[0:C, :] = low.astype(BF)
    ref[C : 2 * C, :] = value.astype(BF)
    ref[2 * C : 3 * C, :] = high.astype(BF)


def compute_kernel(
    share, own, chunk, naz, gates, rays, scale,
    ids_ref, xc_ref, embed_ref, proj_ref, k1_ref, k2_ref, wj_ref, head_ref,
    pred_ref, pay_ref,
    t0, t1, tu2, tu1, pack,
):
    g = gates
    n = rays * g
    nx = xc_ref.shape[1]
    sweeps = embed_ref.shape[0]
    slots = ids_ref.shape[0]

    def put(start, value):
        for src, dst, size in pieces(start, value.shape[0], share, chunk):
            pack[dst : dst + size, :] = value[src : src + size, :]

    def conv(k_ref, taps, first, step, width):
        total = None
        for p in range(3):
            kp = k_ref[p * 3 * C : (p + 1) * 3 * C, :]
            term = dot(kp, taps[:, first + p * step : first + p * step + width], TN)
            total = term if total is None else total + term
        return total

    def back(k_ref, taps, step, width):
        total = None
        for p in range(3):
            m = jnp.concatenate(
                [
                    k_ref[((2 - p) * 3 + 2 - q) * C : ((2 - p) * 3 + 3 - q) * C, :]
                    for q in range(3)
                ],
                axis=1,
            )
            term = dot(m, taps[:, p * step : p * step + width], NN)
            total = term if total is None else total + term
        return total

    pack[...] = jnp.zeros_like(pack)
    owns = []
    row = jnp.zeros((1, C), F32)
    for s in range(sweeps):
        w = jnp.float32(0.0)
        for j in range(slots):
            w = w + jnp.where(ids_ref[j] == s, 1.0, 0.0)
        owns.append(w)
        row = row + w * embed_ref[s : s + 1, :]
    bias = jnp.broadcast_to(row, (C, C)).T[:, 0:1]

    s0 = (dot(proj_ref[...], xc_ref[0:48, :], TN) + bias).astype(BF).astype(F32)
    fill_taps(t0, s0 * logistic(s0), D1, g)

    w1 = (rays + 2 * D2) * g
    s1 = s0[:, D1 * g : D1 * g + w1] + conv(k1_ref, t0, 0, D1 * g, w1)
    s1 = s1.astype(BF).astype(F32)
    fill_taps(t1, s1 * logistic(s1), D2, g)
    s2 = s1[:, D2 * g : D2 * g + n] + conv(k2_ref, t1, 0, D2 * g, n)
    s2 = s2.astype(BF)

    joined = dot(wj_ref[...], s2, TN).astype(BF)
    pred_ref[...] = dot(head_ref[...], joined, NN)

    jb = dot(head_ref[...], xc_ref[48:64, :], TN).astype(BF)
    join = dot(s2, jb[:, HALO * g : HALO * g + n], NT) * scale
    for k in range(naz):
        pack[k * chunk + share : (k + 1) * chunk, :] = join[k * own : (k + 1) * own, :]

    g2 = dot(wj_ref[...], jb, NN)
    fill_taps(tu2, g2, D2, g)
    for p in range(3):
        part = dot(
            t1[:, p * D2 * g : p * D2 * g + n], tu2[C : 2 * C, HALO * g : HALO * g + n], NT
        )
        put((3 + p) * 3 * C, part * scale)

    wb = (rays + 2 * D1) * g
    g1 = g2[:, D2 * g : D2 * g + wb] + back(k2_ref, tu2, D2 * g, wb) * slope(
        s1[:, (D2 - D1) * g : (D2 - D1) * g + wb]
    )
    fill_taps(tu1, g1, D1, g)
    for p in range(3):
        first = (HALO + D1 * (p - 1)) * g
        part = dot(t0[:, first : first + n], tu1[C : 2 * C, D1 * g : D1 * g + n], NT)
        put(p * 3 * C, part * scale)
    g0 = g1[:, D1 * g : D1 * g + n] + back(k1_ref, tu1, D1 * g, n) * slope(
        s0[:, HALO * g : HALO * g + n]
    )
    g0 = g0.astype(BF)
    gin = dot(xc_ref[0:48, HALO * g : HALO * g + n], g0, NT)
    put(18 * C, (gin[0:24, :] + gin[24:48, :]) * scale)
    column = dot(jnp.ones((8, n), BF), g0, NT)[0:1, :] * scale
    lines = up8(sweeps)
    index = lax.broadcasted_iota(jnp.int32, (lines, C), 0)
    grads = jnp.zeros((lines, C), F32)
    for s in range(sweeps):
        grads = grads + jnp.where(index == s, owns[s] * column, 0.0)
    put(18 * C + 24, grads)
    pay_ref[...] = pack[...].astype(BF)


def sum_kernel(
    share, own, chunk, naz, nel,
    pred_in, pay,
    pred_out, join_out, first_out, second_out, input_out, embed_out,
    rbuf, mbuf, gbuf, pbuf,
    s1, r1, s2, r2, s3, r3, sp, rp,
):
    a = lax.axis_index("az")
    e = lax.axis_index("el")
    barrier = pltpu.get_barrier_semaphore()
    for s in range(1, naz):
        pl.semaphore_signal(
            barrier, inc=1, device_id={"az": lax.rem(a + s, naz), "el": e}, device_id_type=MESH
        )
    for t in range(1, nel):
        pl.semaphore_signal(
            barrier, inc=1, device_id={"az": a, "el": lax.rem(e + t, nel)}, device_id_type=MESH
        )
    pl.semaphore_wait(barrier, naz + nel - 2)

    scatter = []
    for s in range(1, naz):
        d = lax.rem(a + s, naz)
        c = pltpu.make_async_remote_copy(
            src_ref=pay.at[pl.ds(pl.multiple_of(d * chunk, 16), chunk), :],
            dst_ref=rbuf.at[s],
            send_sem=s1.at[s],
            recv_sem=r1.at[s],
            device_id={"az": d, "el": e},
            device_id_type=MESH,
        )
        c.start()
        scatter.append(c)
    sends = []
    for t in range(1, nel):
        c = pltpu.make_async_remote_copy(
            src_ref=pred_in,
            dst_ref=pbuf.at[e],
            send_sem=sp.at[t],
            recv_sem=rp.at[t],
            device_id={"az": a, "el": lax.rem(e + t, nel)},
            device_id_type=MESH,
        )
        c.start()
        sends.append(c)
    pbuf[e] = pred_in[...]
    mine = pl.ds(pl.multiple_of(a * chunk, 16), chunk)
    acc = pay[mine, :].astype(F32)
    for s in range(1, naz):
        scatter[s - 1].wait_recv()
        acc = acc + rbuf[s].astype(F32)
    mbuf[e] = acc.astype(BF)
    cross = []
    for t in range(1, nel):
        c = pltpu.make_async_remote_copy(
            src_ref=mbuf.at[e],
            dst_ref=mbuf.at[e],
            send_sem=s2.at[t],
            recv_sem=r2.at[t],
            device_id={"az": a, "el": lax.rem(e + t, nel)},
            device_id_type=MESH,
        )
        c.start()
        cross.append(c)
    for c in cross:
        c.wait_recv()
    total = mbuf[0].astype(F32)
    for t in range(1, nel):
        total = total + mbuf[t].astype(F32)
    line = lax.broadcasted_iota(jnp.int32, total.shape, 0)
    total = jnp.where(line < share, total, acc)
    gbuf[mine, :] = total.astype(BF)
    gather = []
    for s in range(1, naz):
        c = pltpu.make_async_remote_copy(
            src_ref=gbuf.at[mine, :],
            dst_ref=gbuf.at[mine, :],
            send_sem=s3.at[s],
            recv_sem=r3.at[s],
            device_id={"az": lax.rem(a + s, naz), "el": e},
            device_id_type=MESH,
        )
        c.start()
        gather.append(c)
    for c in sends:
        c.wait_recv()
    leads = pred_out.shape[0]
    pred = pbuf[0]
    for t in range(1, nel):
        pred = pred + pbuf[t]
    pred_out[...] = pred[0:leads, :]
    for c in gather:
        c.wait_recv()

    def take(ref, start):
        for dst, src, size in pieces(start, ref.shape[0], share, chunk):
            ref[dst : dst + size, :] = gbuf[src : src + size, :].astype(F32)

    take(first_out, 0)
    take(second_out, 9 * C)
    take(input_out, 18 * C)
    take(embed_out, 18 * C + 24)
    for k in range(naz):
        join_out[k * own : (k + 1) * own, :] = gbuf[
            k * chunk + share : (k + 1) * chunk, :
        ].astype(F32)
    for c in scatter + sends + cross + gather:
        c.wait_send()


def shards(
    raw_sweeps, sweep_ids, elevation_embed, input_proj, first_kernel, second_kernel,
    join_weight, head_weight, cotangent,
):
    naz = lax.axis_size("az")
    nel = lax.axis_size("el")
    slots, _, inputs, rays, gates = raw_sweeps.shape
    leads = head_weight.shape[0]
    sweeps = elevation_embed.shape[0]
    share, own, chunk = layout(sweeps, naz)
    scale = 1.0 / math.sqrt(nel * rays * naz * gates)
    n = rays * gates
    h = HALO * gates

    xc = jnp.concatenate(
        [
            raw_sweeps.reshape(slots * inputs, n),
            cotangent.reshape(leads, n),
            jnp.zeros((16 - leads, n), BF),
        ],
        axis=0,
    )
    forward = [(i, (i + 1) % naz) for i in range(naz)]
    backward = [(t, s) for s, t in forward]
    low = lax.ppermute(xc[:, n - h :], "az", forward)
    high = lax.ppermute(xc[:, :h], "az", backward)
    xc = jnp.concatenate([low, xc, high], axis=1)
    proj = jnp.concatenate([input_proj] * slots, axis=0)
    head = jnp.pad(head_weight, ((0, 16 - leads), (0, 0)))
    vm = pl.BlockSpec(memory_space=pltpu.VMEM)
    total = naz * chunk
    pred, pay = pl.pallas_call(
        functools.partial(compute_kernel, share, own, chunk, naz, gates, rays, scale),
        out_shape=(
            jax.ShapeDtypeStruct((16, n), F32),
            jax.ShapeDtypeStruct((total, C), BF),
        ),
        in_specs=[pl.BlockSpec(memory_space=pltpu.SMEM)] + [vm] * 7,
        out_specs=(vm, vm),
        scratch_shapes=[
            pltpu.VMEM((3 * C, n + 2 * h), BF),
            pltpu.VMEM((3 * C, (rays + 2 * D2) * gates), BF),
            pltpu.VMEM((3 * C, n + 2 * h), BF),
            pltpu.VMEM((3 * C, (rays + 2 * D1) * gates), BF),
            pltpu.VMEM((total, C), F32),
        ],
        compiler_params=pltpu.CompilerParams(vmem_limit_bytes=48 * 1024 * 1024),
        name="step_compute",
    )(
        sweep_ids, xc, elevation_embed, proj,
        first_kernel.reshape(9 * C, C), second_kernel.reshape(9 * C, C),
        join_weight[0], head,
    )
    dma = pltpu.SemaphoreType.DMA
    pred, join, first, second, gin, emb = pl.pallas_call(
        functools.partial(sum_kernel, share, own, chunk, naz, nel),
        out_shape=(
            jax.ShapeDtypeStruct((leads, n), F32),
            jax.ShapeDtypeStruct((C, C), F32),
            jax.ShapeDtypeStruct((9 * C, C), F32),
            jax.ShapeDtypeStruct((9 * C, C), F32),
            jax.ShapeDtypeStruct((inputs, C), F32),
            jax.ShapeDtypeStruct((sweeps, C), F32),
        ),
        in_specs=[vm, vm],
        out_specs=(vm,) * 6,
        scratch_shapes=[
            pltpu.VMEM((naz, chunk, C), BF),
            pltpu.VMEM((nel, chunk, C), BF),
            pltpu.VMEM((total, C), BF),
            pltpu.VMEM((nel, 16, n), F32),
            dma((naz,)), dma((naz,)), dma((nel,)), dma((nel,)),
            dma((naz,)), dma((naz,)), dma((nel,)), dma((nel,)),
        ],
        compiler_params=pltpu.CompilerParams(collective_id=0, has_side_effects=True),
        name="step_sum",
    )(pred, pay)
    shape = first_kernel.shape
    return (
        pred.reshape(1, leads, rays, gates),
        join[None],
        first.reshape(shape),
        second.reshape(shape),
        gin,
        emb,
    )


def solution(mesh):
    in_specs = (
        P("el", None, None, "az", None),
        P("el"),
        P(),
        P(),
        P(),
        P(),
        P("el", None, None),
        P(),
        P(None, None, "az", None),
    )
    out_specs = (P(None, None, "az", None), P("el", None, None), P(), P(), P(), P())
    return jax.shard_map(shards, mesh=mesh, in_specs=in_specs, out_specs=out_specs, check_vma=False)
```

```python
import functools
import math

import jax
import jax.numpy as jnp
from jax import lax
from jax.experimental import pallas as pl
from jax.experimental.pallas import tpu as pltpu
from jax.sharding import PartitionSpec as P

C = 128
D1 = 1
D2 = 2
HALO = D1 + D2
BF = jnp.bfloat16
F32 = jnp.float32
MESH = pl.DeviceIdType.MESH
NN = (((1,), (0,)), ((), ()))
NT = (((1,), (1,)), ((), ()))
TN = (((0,), (0,)), ((), ()))


def dot(a, b, dims):
    return lax.dot_general(a, b, dims, preferred_element_type=F32)


def up8(n):
    return -(-n // 8) * 8


def up16(n):
    return -(-n // 16) * 16


def logistic(v):
    return 1.0 / (1.0 + jnp.exp(-v))


def slope(v):
    s = logistic(v)
    return s * (1.0 + v * (1.0 - s))


def layouts(sweeps, naz):
    own = C // naz
    share = up8(-(-9 * C // naz))
    chunk = up16(share + own)
    rest = up16(-(-(9 * C + 24 + up8(sweeps)) // naz))
    return (chunk - own, own, chunk), (rest, 0, rest)


def pieces(start, count, share, chunk):
    out = []
    done = 0
    while done < count:
        k, off = divmod(start + done, share)
        size = min(count - done, share - off)
        out.append((done, k * chunk + off, size))
        done += size
    return out


def fill_taps(ref, value, dilate, gates):
    n = value.shape[1]
    gate = lax.broadcasted_iota(jnp.int32, value.shape, 1) % gates
    low = jnp.where(gate >= dilate, pltpu.roll(value, dilate, 1), 0.0)
    high = jnp.where(gate < gates - dilate, pltpu.roll(value, n - dilate, 1), 0.0)
    ref[0:C, :] = low.astype(BF)
    ref[C : 2 * C, :] = value.astype(BF)
    ref[2 * C : 3 * C, :] = high.astype(BF)


def step_kernel(
    parts, naz, nel, gates, rays, scale,
    ids_ref, xc_ref, embed_ref, proj_ref, k1_ref, k2_ref, wj_ref, head_ref,
    pred_out, join_out, first_out, second_out, input_out, embed_out,
    xe, t0, t1, tu2, tu1,
    pack0, pack1, pay0, pay1, abuf0, abuf1, half0, half1,
    rbuf0, rbuf1, mbuf0, mbuf1, gbuf0, gbuf1, pbuf,
    sh, rh, sa, ra, sb, rb, sc, rc, sd, rd, se, re, sp, rp,
):
    packs, pays, abufs, halves = (pack0, pack1), (pay0, pay1), (abuf0, abuf1), (half0, half1)
    rbufs, mbufs, gbufs = (rbuf0, rbuf1), (mbuf0, mbuf1), (gbuf0, gbuf1)
    g = gates
    n = rays * g
    h = HALO * g
    sweeps = embed_ref.shape[0]
    slots = ids_ref.shape[0]
    nq = naz // 2
    a = lax.axis_index("az")
    e = lax.axis_index("el")
    core = lax.rem(a, 2)
    q = a // 2
    started = []

    def at(az, el):
        return {"az": az, "el": el}

    partner = at(a + 1 - 2 * core, e)
    right = at(lax.rem(a + 1, naz), e)
    left = at(lax.rem(a + naz - 1, naz), e)
    same = [at(2 * lax.rem(q + s, nq) + core, e) for s in range(nq)]
    column = [at(a, lax.rem(e + t, nel)) for t in range(nel)]

    barrier = pltpu.get_barrier_semaphore()
    greeted = [partner, right, left] + same[1:] + column[1:]
    for device in greeted:
        pl.semaphore_signal(barrier, inc=1, device_id=device, device_id_type=MESH)
    xe[:, h : h + n] = xc_ref[...]
    pl.semaphore_wait(barrier, len(greeted))

    def send(source, target, ssem, rsem, device):
        c = pltpu.make_async_remote_copy(
            src_ref=source, dst_ref=target, send_sem=ssem, recv_sem=rsem,
            device_id=device, device_id_type=MESH,
        )
        c.start()
        started.append(c)
        return c

    up = send(xc_ref.at[:, n - h : n], xe.at[:, 0:h], sh.at[0], rh.at[0], right)
    down = send(xc_ref.at[:, 0:h], xe.at[:, h + n : n + 2 * h], sh.at[1], rh.at[1], left)

    def rows(index, chunk):
        return pl.ds(pl.multiple_of(index * chunk, 16), chunk)

    def put(i, start, value):
        share, own, chunk = parts[i]
        for src, dst, size in pieces(start, value.shape[0], share, chunk):
            packs[i][dst : dst + size, :] = value[src : src + size, :]

    def phase_a(i):
        chunk = parts[i][2]
        pays[i][...] = packs[i][...].astype(BF)
        return send(
            pays[i].at[rows(1 - core, nq * chunk), :], abufs[i], sa.at[i], ra.at[i], partner
        )

    def phase_b(i, arrived):
        chunk = parts[i][2]
        arrived.wait_recv()
        mine = pays[i][rows(core, nq * chunk), :].astype(F32)
        halves[i][...] = (mine + abufs[i][...].astype(F32)).astype(BF)
        return [
            send(
                halves[i].at[rows(lax.rem(q + s, nq), chunk), :], rbufs[i].at[s],
                sb.at[i, s], rb.at[i, s], same[s],
            )
            for s in range(1, nq)
        ]

    def phase_c(i, arrived):
        chunk = parts[i][2]
        acc = halves[i][rows(q, chunk), :].astype(F32)
        for s in range(1, nq):
            arrived[s - 1].wait_recv()
            acc = acc + rbufs[i][s].astype(F32)
        mbufs[i][e] = acc.astype(BF)
        sent = [
            send(mbufs[i].at[e], mbufs[i].at[e], sc.at[i, t], rc.at[i, t], column[t])
            for t in range(1, nel)
        ]
        return acc, sent

    def phase_d(i, acc, arrived):
        share, own, chunk = parts[i]
        for c in arrived:
            c.wait_recv()
        total = mbufs[i][0].astype(F32)
        for t in range(1, nel):
            total = total + mbufs[i][t].astype(F32)
        if own:
            line = lax.broadcasted_iota(jnp.int32, total.shape, 0)
            total = jnp.where(line < share, total, acc)
        mine = rows(core * nq + q, chunk)
        gbufs[i][mine, :] = total.astype(BF)
        view = gbufs[i].at[mine, :]
        sent = [send(view, view, sd.at[i, s], rd.at[i, s], same[s]) for s in range(1, nq)]
        own_sent = send(view, view, se.at[i, 0], re.at[i, 0], partner)
        return sent, own_sent

    def phase_e(i, arrived, own_sent):
        chunk = parts[i][2]
        last = [own_sent]
        for s in range(1, nq):
            arrived[s - 1].wait_recv()
            view = gbufs[i].at[rows(core * nq + lax.rem(q + nq - s, nq), chunk), :]
            last.append(send(view, view, se.at[i, s], re.at[i, s], partner))
        return last

    def take(i, ref, start):
        share, own, chunk = parts[i]
        for dst, src, size in pieces(start, ref.shape[0], share, chunk):
            ref[dst : dst + size, :] = gbufs[i][src : src + size, :].astype(F32)

    def conv(k_ref, taps, first, step, width):
        total = None
        for p in range(3):
            kp = k_ref[p * 3 * C : (p + 1) * 3 * C, :]
            term = dot(kp, taps[:, first + p * step : first + p * step + width], TN)
            total = term if total is None else total + term
        return total

    def back(k_ref, taps, step, width):
        total = None
        for p in range(3):
            m = jnp.concatenate(
                [
                    k_ref[((2 - p) * 3 + 2 - q_) * C : ((2 - p) * 3 + 3 - q_) * C, :]
                    for q_ in range(3)
                ],
                axis=1,
            )
            term = dot(m, taps[:, p * step : p * step + width], NN)
            total = term if total is None else total + term
        return total

    packs[0][...] = jnp.zeros_like(packs[0])
    packs[1][...] = jnp.zeros_like(packs[1])
    owns = []
    row = jnp.zeros((1, C), F32)
    for s in range(sweeps):
        w = jnp.float32(0.0)
        for j in range(slots):
            w = w + jnp.where(ids_ref[j] == s, 1.0, 0.0)
        owns.append(w)
        row = row + w * embed_ref[s : s + 1, :]
    bias = jnp.broadcast_to(row, (C, C)).T[:, 0:1]

    up.wait_recv()
    down.wait_recv()
    s0 = (dot(proj_ref[...], xe[0:48, :], TN) + bias).astype(BF).astype(F32)
    fill_taps(t0, s0 * logistic(s0), D1, g)

    w1 = (rays + 2 * D2) * g
    s1 = s0[:, D1 * g : D1 * g + w1] + conv(k1_ref, t0, 0, D1 * g, w1)
    s1 = s1.astype(BF).astype(F32)
    fill_taps(t1, s1 * logistic(s1), D2, g)
    s2 = s1[:, D2 * g : D2 * g + n] + conv(k2_ref, t1, 0, D2 * g, n)
    s2 = s2.astype(BF)

    jb = dot(head_ref[...], xe[48:64, :], TN).astype(BF)
    join = dot(s2, jb[:, HALO * g : HALO * g + n], NT) * scale
    share, own, chunk = parts[0]
    for k in range(naz):
        packs[0][k * chunk + share : (k + 1) * chunk, :] = join[k * own : (k + 1) * own, :]

    g2 = dot(wj_ref[...], jb, NN)
    fill_taps(tu2, g2, D2, g)
    for p in range(3):
        part = dot(
            t1[:, p * D2 * g : p * D2 * g + n], tu2[C : 2 * C, HALO * g : HALO * g + n], NT
        )
        put(0, p * 3 * C, part * scale)
    a0 = phase_a(0)

    joined = dot(wj_ref[...], s2, TN).astype(BF)
    pbuf[e] = dot(head_ref[...], joined, NN)

    wb = (rays + 2 * D1) * g
    g1 = g2[:, D2 * g : D2 * g + wb] + back(k2_ref, tu2, D2 * g, wb) * slope(
        s1[:, (D2 - D1) * g : (D2 - D1) * g + wb]
    )
    b0 = phase_b(0, a0)
    fill_taps(tu1, g1, D1, g)
    for p in range(3):
        first = (HALO + D1 * (p - 1)) * g
        part = dot(t0[:, first : first + n], tu1[C : 2 * C, D1 * g : D1 * g + n], NT)
        put(1, p * 3 * C, part * scale)
    g0 = g1[:, D1 * g : D1 * g + n] + back(k1_ref, tu1, D1 * g, n) * slope(
        s0[:, HALO * g : HALO * g + n]
    )
    g0 = g0.astype(BF)
    gin = dot(xe[0:48, HALO * g : HALO * g + n], g0, NT)
    put(1, 9 * C, (gin[0:24, :] + gin[24:48, :]) * scale)
    summed = dot(jnp.ones((8, n), BF), g0, NT)[0:1, :] * scale
    lines = up8(sweeps)
    index = lax.broadcasted_iota(jnp.int32, (lines, C), 0)
    grads = jnp.zeros((lines, C), F32)
    for s in range(sweeps):
        grads = grads + jnp.where(index == s, owns[s] * summed, 0.0)
    put(1, 9 * C + 24, grads)
    a1 = phase_a(1)
    acc0, c0 = phase_c(0, b0)
    b1 = phase_b(1, a1)
    d0, own0 = phase_d(0, acc0, c0)
    preds = [
        send(pbuf.at[e], pbuf.at[e], sp.at[t], rp.at[t], column[t]) for t in range(1, nel)
    ]
    acc1, c1 = phase_c(1, b1)
    d1, own1 = phase_d(1, acc1, c1)
    e0 = phase_e(0, d0, own0)
    for c in preds:
        c.wait_recv()
    pred = pbuf[0]
    for t in range(1, nel):
        pred = pred + pbuf[t]
    pred_out[...] = pred[0 : pred_out.shape[0], :]
    for c in e0:
        c.wait_recv()
    take(0, second_out, 0)
    for k in range(naz):
        join_out[k * own : (k + 1) * own, :] = gbufs[0][
            k * chunk + share : (k + 1) * chunk, :
        ].astype(F32)
    e1 = phase_e(1, d1, own1)
    for c in e1:
        c.wait_recv()
    take(1, first_out, 0)
    take(1, input_out, 9 * C)
    take(1, embed_out, 9 * C + 24)
    for c in started:
        c.wait_send()


def shards(
    raw_sweeps, sweep_ids, elevation_embed, input_proj, first_kernel, second_kernel,
    join_weight, head_weight, cotangent,
):
    naz = lax.axis_size("az")
    nel = lax.axis_size("el")
    slots, _, inputs, rays, gates = raw_sweeps.shape
    leads = head_weight.shape[0]
    sweeps = elevation_embed.shape[0]
    parts = layouts(sweeps, naz)
    scale = 1.0 / math.sqrt(nel * rays * naz * gates)
    n = rays * gates
    h = HALO * gates
    nq = naz // 2

    xc = jnp.concatenate(
        [
            raw_sweeps.reshape(slots * inputs, n),
            cotangent.reshape(leads, n),
            jnp.zeros((16 - leads, n), BF),
        ],
        axis=0,
    )
    proj = jnp.concatenate([input_proj] * slots, axis=0)
    head = jnp.pad(head_weight, ((0, 16 - leads), (0, 0)))
    vm = pl.BlockSpec(memory_space=pltpu.VMEM)
    dma = pltpu.SemaphoreType.DMA

    def both(shape, kind=BF):
        return [pltpu.VMEM(shape(chunk), kind) for _, _, chunk in parts]

    pred, join, first, second, gin, emb = pl.pallas_call(
        functools.partial(step_kernel, parts, naz, nel, gates, rays, scale),
        out_shape=(
            jax.ShapeDtypeStruct((leads, n), F32),
            jax.ShapeDtypeStruct((C, C), F32),
            jax.ShapeDtypeStruct((9 * C, C), F32),
            jax.ShapeDtypeStruct((9 * C, C), F32),
            jax.ShapeDtypeStruct((inputs, C), F32),
            jax.ShapeDtypeStruct((sweeps, C), F32),
        ),
        in_specs=[pl.BlockSpec(memory_space=pltpu.SMEM)] + [vm] * 7,
        out_specs=(vm,) * 6,
        scratch_shapes=[
            pltpu.VMEM((64, n + 2 * h), BF),
            pltpu.VMEM((3 * C, n + 2 * h), BF),
            pltpu.VMEM((3 * C, (rays + 2 * D2) * gates), BF),
            pltpu.VMEM((3 * C, n + 2 * h), BF),
            pltpu.VMEM((3 * C, (rays + 2 * D1) * gates), BF),
        ]
        + both(lambda chunk: (naz * chunk, C), F32)
        + both(lambda chunk: (naz * chunk, C))
        + both(lambda chunk: (nq * chunk, C))
        + both(lambda chunk: (nq * chunk, C))
        + both(lambda chunk: (nq, chunk, C))
        + both(lambda chunk: (nel, chunk, C))
        + both(lambda chunk: (naz * chunk, C))
        + [
            pltpu.VMEM((nel, 16, n), F32),
            dma((2,)), dma((2,)),
            dma((2,)), dma((2,)),
            dma((2, nq)), dma((2, nq)),
            dma((2, nel)), dma((2, nel)),
            dma((2, nq)), dma((2, nq)),
            dma((2, nq)), dma((2, nq)),
            dma((nel,)), dma((nel,)),
        ],
        compiler_params=pltpu.CompilerParams(
            collective_id=0, has_side_effects=True, vmem_limit_bytes=48 * 1024 * 1024
        ),
        name="step",
    )(
        sweep_ids, xc, elevation_embed, proj,
        first_kernel.reshape(9 * C, C), second_kernel.reshape(9 * C, C),
        join_weight[0], head,
    )
    shape = first_kernel.shape
    return (
        pred.reshape(1, leads, rays, gates),
        join[None],
        first.reshape(shape),
        second.reshape(shape),
        gin,
        emb,
    )


def solution(mesh):
    in_specs = (
        P("el", None, None, "az", None),
        P("el"),
        P(),
        P(),
        P(),
        P(),
        P("el", None, None),
        P(),
        P(None, None, "az", None),
    )
    out_specs = (P(None, None, "az", None), P("el", None, None), P(), P(), P(), P())
    return jax.shard_map(shards, mesh=mesh, in_specs=in_specs, out_specs=out_specs, check_vma=False)
```

```python
import functools
import math

import jax
import jax.numpy as jnp
from jax import lax
from jax.experimental import pallas as pl
from jax.experimental.pallas import tpu as pltpu
from jax.sharding import PartitionSpec as P

C = 128
D1 = 1
D2 = 2
HALO = D1 + D2
BF = jnp.bfloat16
F32 = jnp.float32
MESH = pl.DeviceIdType.MESH
NN = (((1,), (0,)), ((), ()))
NT = (((1,), (1,)), ((), ()))
TN = (((0,), (0,)), ((), ()))


def dot(a, b, dims):
    return lax.dot_general(a, b, dims, preferred_element_type=F32)


def up8(n):
    return -(-n // 8) * 8


def up16(n):
    return -(-n // 16) * 16


def logistic(v):
    return 1.0 / (1.0 + jnp.exp(-v))


def slope(v):
    s = logistic(v)
    return s * (1.0 + v * (1.0 - s))


def layouts(sweeps, naz):
    own = C // naz
    share = up8(-(-9 * C // naz))
    chunk = up16(share + own)
    rest = up16(-(-(9 * C + 24 + up8(sweeps)) // naz))
    return (chunk - own, own, chunk), (rest, 0, rest)


def pieces(start, count, share, chunk):
    out = []
    done = 0
    while done < count:
        k, off = divmod(start + done, share)
        size = min(count - done, share - off)
        out.append((done, k * chunk + off, size))
        done += size
    return out


def fill_taps(ref, value, dilate, gates):
    n = value.shape[1]
    gate = lax.broadcasted_iota(jnp.int32, value.shape, 1) % gates
    low = jnp.where(gate >= dilate, pltpu.roll(value, dilate, 1), 0.0)
    high = jnp.where(gate < gates - dilate, pltpu.roll(value, n - dilate, 1), 0.0)
    ref[0:C, :] = low.astype(BF)
    ref[C : 2 * C, :] = value.astype(BF)
    ref[2 * C : 3 * C, :] = high.astype(BF)


def step_kernel(
    parts, naz, nel, gates, rays, scale,
    ids_ref, xc_ref, embed_ref, proj_ref, k1_ref, k2_ref, wj_ref, head_ref,
    pred_out, join_out, first_out, second_out, input_out, embed_out,
    xe, t0, t1, tu2, tu1,
    pack0, pack1, pay0, pay1, abuf0, abuf1, half0, half1,
    rbuf0, rbuf1, mbuf0, mbuf1, gbuf0, gbuf1, pbuf,
    sh, rh, sa, ra, sb, rb, sc, rc, sd, rd, se, re, sp, rp,
):
    packs, pays, abufs, halves = (pack0, pack1), (pay0, pay1), (abuf0, abuf1), (half0, half1)
    rbufs, mbufs, gbufs = (rbuf0, rbuf1), (mbuf0, mbuf1), (gbuf0, gbuf1)
    g = gates
    n = rays * g
    h = HALO * g
    sweeps = embed_ref.shape[0]
    slots = ids_ref.shape[0]
    nq = naz // 2
    a = lax.axis_index("az")
    e = lax.axis_index("el")
    core = lax.rem(a, 2)
    q = a // 2
    started = []

    def at(az, el):
        return {"az": az, "el": el}

    partner = at(a + 1 - 2 * core, e)
    right = at(lax.rem(a + 1, naz), e)
    left = at(lax.rem(a + naz - 1, naz), e)
    same = [at(2 * lax.rem(q + s, nq) + core, e) for s in range(nq)]
    column = [at(a, lax.rem(e + t, nel)) for t in range(nel)]

    barrier = pltpu.get_barrier_semaphore()
    greeted = [partner, right, left] + same[1:] + column[1:]
    for device in greeted:
        pl.semaphore_signal(barrier, inc=1, device_id=device, device_id_type=MESH)
    xe[:, h : h + n] = xc_ref[...]
    pl.semaphore_wait(barrier, len(greeted))

    def send(source, target, ssem, rsem, device):
        c = pltpu.make_async_remote_copy(
            src_ref=source, dst_ref=target, send_sem=ssem, recv_sem=rsem,
            device_id=device, device_id_type=MESH,
        )
        c.start()
        started.append(c)
        return c

    up = send(xc_ref.at[:, n - h : n], xe.at[:, 0:h], sh.at[0], rh.at[0], right)
    down = send(xc_ref.at[:, 0:h], xe.at[:, h + n : n + 2 * h], sh.at[1], rh.at[1], left)

    def rows(index, chunk):
        return pl.ds(pl.multiple_of(index * chunk, 16), chunk)

    def put(i, start, value):
        share, own, chunk = parts[i]
        for src, dst, size in pieces(start, value.shape[0], share, chunk):
            packs[i][dst : dst + size, :] = value[src : src + size, :]

    def phase_a(i):
        chunk = parts[i][2]
        pays[i][...] = packs[i][...].astype(BF)
        return send(
            pays[i].at[rows(1 - core, nq * chunk), :], abufs[i], sa.at[i], ra.at[i], partner
        )

    def phase_b(i, arrived):
        chunk = parts[i][2]
        arrived.wait_recv()
        mine = pays[i][rows(core, nq * chunk), :].astype(F32)
        halves[i][...] = (mine + abufs[i][...].astype(F32)).astype(BF)
        return [
            send(
                halves[i].at[rows(lax.rem(q + s, nq), chunk), :], rbufs[i].at[s],
                sb.at[i, s], rb.at[i, s], same[s],
            )
            for s in range(1, nq)
        ]

    def phase_c(i, arrived):
        chunk = parts[i][2]
        acc = halves[i][rows(q, chunk), :].astype(F32)
        for s in range(1, nq):
            arrived[s - 1].wait_recv()
            acc = acc + rbufs[i][s].astype(F32)
        mbufs[i][e] = acc.astype(BF)
        sent = [
            send(mbufs[i].at[e], mbufs[i].at[e], sc.at[i, t], rc.at[i, t], column[t])
            for t in range(1, nel)
        ]
        return acc, sent

    def phase_d(i, acc, arrived):
        share, own, chunk = parts[i]
        for c in arrived:
            c.wait_recv()
        total = mbufs[i][0].astype(F32)
        for t in range(1, nel):
            total = total + mbufs[i][t].astype(F32)
        if own:
            line = lax.broadcasted_iota(jnp.int32, total.shape, 0)
            total = jnp.where(line < share, total, acc)
        mine = rows(core * nq + q, chunk)
        gbufs[i][mine, :] = total.astype(BF)
        view = gbufs[i].at[mine, :]
        sent = [send(view, view, sd.at[i, s], rd.at[i, s], same[s]) for s in range(1, nq)]
        own_sent = send(view, view, se.at[i, 0], re.at[i, 0], partner)
        return sent, own_sent

    def phase_e(i, arrived, own_sent):
        chunk = parts[i][2]
        last = [own_sent]
        for s in range(1, nq):
            arrived[s - 1].wait_recv()
            view = gbufs[i].at[rows(core * nq + lax.rem(q + nq - s, nq), chunk), :]
            last.append(send(view, view, se.at[i, s], re.at[i, s], partner))
        return last

    def take(i, ref, start):
        share, own, chunk = parts[i]
        for dst, src, size in pieces(start, ref.shape[0], share, chunk):
            ref[dst : dst + size, :] = gbufs[i][src : src + size, :].astype(F32)

    def conv(k_ref, taps, first, step, width):
        total = None
        for p in range(3):
            kp = k_ref[p * 3 * C : (p + 1) * 3 * C, :]
            term = dot(kp, taps[:, first + p * step : first + p * step + width], TN)
            total = term if total is None else total + term
        return total

    def back(k_ref, taps, step, width):
        total = None
        for p in range(3):
            m = jnp.concatenate(
                [
                    k_ref[((2 - p) * 3 + 2 - q_) * C : ((2 - p) * 3 + 3 - q_) * C, :]
                    for q_ in range(3)
                ],
                axis=1,
            )
            term = dot(m, taps[:, p * step : p * step + width], NN)
            total = term if total is None else total + term
        return total

    packs[0][...] = jnp.zeros_like(packs[0])
    packs[1][...] = jnp.zeros_like(packs[1])
    owns = []
    row = jnp.zeros((1, C), F32)
    for s in range(sweeps):
        w = jnp.float32(0.0)
        for j in range(slots):
            w = w + jnp.where(ids_ref[j] == s, 1.0, 0.0)
        owns.append(w)
        row = row + w * embed_ref[s : s + 1, :]
    bias = jnp.broadcast_to(row, (C, C)).T[:, 0:1]

    up.wait_recv()
    down.wait_recv()
    proj = proj_ref[...].astype(F32)
    proj = jnp.concatenate([proj] * slots, axis=0).astype(BF)
    s0 = (dot(proj, xe[0:48, :], TN) + bias).astype(BF).astype(F32)
    fill_taps(t0, s0 * logistic(s0), D1, g)

    w1 = (rays + 2 * D2) * g
    s1 = s0[:, D1 * g : D1 * g + w1] + conv(k1_ref, t0, 0, D1 * g, w1)
    s1 = s1.astype(BF).astype(F32)
    fill_taps(t1, s1 * logistic(s1), D2, g)
    s2 = s1[:, D2 * g : D2 * g + n] + conv(k2_ref, t1, 0, D2 * g, n)
    s2 = s2.astype(BF)

    jb = dot(head_ref[...], xe[48:60, :], TN).astype(BF)
    join = dot(s2, jb[:, HALO * g : HALO * g + n], NT) * scale
    share, own, chunk = parts[0]
    for k in range(naz):
        packs[0][k * chunk + share : (k + 1) * chunk, :] = join[k * own : (k + 1) * own, :]

    g2 = dot(wj_ref[...], jb, NN)
    fill_taps(tu2, g2, D2, g)
    for p in range(3):
        part = dot(
            t1[:, p * D2 * g : p * D2 * g + n], tu2[C : 2 * C, HALO * g : HALO * g + n], NT
        )
        put(0, p * 3 * C, part * scale)
    a0 = phase_a(0)

    joined = dot(wj_ref[...], s2, TN).astype(BF)
    pbuf[e] = dot(head_ref[...], joined, NN)

    wb = (rays + 2 * D1) * g
    g1 = g2[:, D2 * g : D2 * g + wb] + back(k2_ref, tu2, D2 * g, wb) * slope(
        s1[:, (D2 - D1) * g : (D2 - D1) * g + wb]
    )
    b0 = phase_b(0, a0)
    fill_taps(tu1, g1, D1, g)
    for p in range(3):
        first = (HALO + D1 * (p - 1)) * g
        part = dot(t0[:, first : first + n], tu1[C : 2 * C, D1 * g : D1 * g + n], NT)
        put(1, p * 3 * C, part * scale)
    g0 = g1[:, D1 * g : D1 * g + n] + back(k1_ref, tu1, D1 * g, n) * slope(
        s0[:, HALO * g : HALO * g + n]
    )
    g0 = g0.astype(BF)
    gin = dot(xe[0:48, HALO * g : HALO * g + n], g0, NT)
    put(1, 9 * C, (gin[0:24, :] + gin[24:48, :]) * scale)
    summed = dot(jnp.ones((8, n), BF), g0, NT)[0:1, :] * scale
    lines = up8(sweeps)
    index = lax.broadcasted_iota(jnp.int32, (lines, C), 0)
    grads = jnp.zeros((lines, C), F32)
    for s in range(sweeps):
        grads = grads + jnp.where(index == s, owns[s] * summed, 0.0)
    put(1, 9 * C + 24, grads)
    a1 = phase_a(1)
    acc0, c0 = phase_c(0, b0)
    b1 = phase_b(1, a1)
    d0, own0 = phase_d(0, acc0, c0)
    preds = [
        send(pbuf.at[e], pbuf.at[e], sp.at[t], rp.at[t], column[t]) for t in range(1, nel)
    ]
    acc1, c1 = phase_c(1, b1)
    d1, own1 = phase_d(1, acc1, c1)
    e0 = phase_e(0, d0, own0)
    for c in preds:
        c.wait_recv()
    pred = pbuf[0]
    for t in range(1, nel):
        pred = pred + pbuf[t]
    pred_out[...] = pred
    for c in e0:
        c.wait_recv()
    take(0, second_out, 0)
    for k in range(naz):
        join_out[k * own : (k + 1) * own, :] = gbufs[0][
            k * chunk + share : (k + 1) * chunk, :
        ].astype(F32)
    e1 = phase_e(1, d1, own1)
    for c in e1:
        c.wait_recv()
    take(1, first_out, 0)
    take(1, input_out, 9 * C)
    take(1, embed_out, 9 * C + 24)
    for c in started:
        c.wait_send()


def write_kernel(*refs):
    ins, outs, (lines, sems) = refs[0:6], refs[6:12], refs[12:14]
    copies = [pltpu.make_async_copy(ins[i], outs[i], sems.at[i]) for i in range(1, 6)]
    for c in copies:
        c.start()
    leads, n = ins[0].shape
    tiles = n // C
    for t in range(tiles):
        lines[pl.ds(t, leads, stride=tiles), :] = ins[0][:, t * C : (t + 1) * C]
    last = pltpu.make_async_copy(lines, outs[0], sems.at[0])
    last.start()
    for c in copies:
        c.wait()
    last.wait()


def shards(
    raw_sweeps, sweep_ids, elevation_embed, input_proj, first_kernel, second_kernel,
    join_weight, head_weight, cotangent,
):
    naz = lax.axis_size("az")
    nel = lax.axis_size("el")
    slots, _, inputs, rays, gates = raw_sweeps.shape
    leads = head_weight.shape[0]
    sweeps = elevation_embed.shape[0]
    parts = layouts(sweeps, naz)
    scale = 1.0 / math.sqrt(nel * rays * naz * gates)
    n = rays * gates
    h = HALO * gates
    nq = naz // 2

    xc = jnp.concatenate(
        [
            raw_sweeps.reshape(slots * inputs, n),
            cotangent.reshape(leads, n),
        ],
        axis=0,
    )
    vm = pl.BlockSpec(memory_space=pltpu.VMEM)
    dma = pltpu.SemaphoreType.DMA

    def both(shape, kind=BF):
        return [pltpu.VMEM(shape(chunk), kind) for _, _, chunk in parts]

    pred, join, first, second, gin, emb = pl.pallas_call(
        functools.partial(step_kernel, parts, naz, nel, gates, rays, scale),
        out_shape=(
            jax.ShapeDtypeStruct((leads, n), F32),
            jax.ShapeDtypeStruct((C, C), F32),
            jax.ShapeDtypeStruct((9 * C, C), F32),
            jax.ShapeDtypeStruct((9 * C, C), F32),
            jax.ShapeDtypeStruct((inputs, C), F32),
            jax.ShapeDtypeStruct((sweeps, C), F32),
        ),
        in_specs=[pl.BlockSpec(memory_space=pltpu.SMEM)] + [vm] * 7,
        out_specs=(vm,) * 6,
        scratch_shapes=[
            pltpu.VMEM((60, n + 2 * h), BF),
            pltpu.VMEM((3 * C, n + 2 * h), BF),
            pltpu.VMEM((3 * C, (rays + 2 * D2) * gates), BF),
            pltpu.VMEM((3 * C, n + 2 * h), BF),
            pltpu.VMEM((3 * C, (rays + 2 * D1) * gates), BF),
        ]
        + both(lambda chunk: (naz * chunk, C), F32)
        + both(lambda chunk: (naz * chunk, C))
        + both(lambda chunk: (nq * chunk, C))
        + both(lambda chunk: (nq * chunk, C))
        + both(lambda chunk: (nq, chunk, C))
        + both(lambda chunk: (nel, chunk, C))
        + both(lambda chunk: (naz * chunk, C))
        + [
            pltpu.VMEM((nel, leads, n), F32),
            dma((2,)), dma((2,)),
            dma((2,)), dma((2,)),
            dma((2, nq)), dma((2, nq)),
            dma((2, nel)), dma((2, nel)),
            dma((2, nq)), dma((2, nq)),
            dma((2, nq)), dma((2, nq)),
            dma((nel,)), dma((nel,)),
        ],
        compiler_params=pltpu.CompilerParams(
            collective_id=0, has_side_effects=True, vmem_limit_bytes=48 * 1024 * 1024
        ),
        name="step",
    )(
        sweep_ids, xc, elevation_embed, input_proj,
        first_kernel.reshape(9 * C, C), second_kernel.reshape(9 * C, C),
        join_weight[0], head_weight,
    )
    tiles = n // C
    arrays = (pred, join, first, second, gin, emb)
    kinds = [jax.ShapeDtypeStruct((leads * tiles, C), F32)]
    kinds += [jax.ShapeDtypeStruct(v.shape, F32) for v in arrays[1:]]
    pred, join, first, second, gin, emb = pl.pallas_call(
        write_kernel,
        out_shape=tuple(kinds),
        in_specs=[vm] * 6,
        out_specs=(pl.BlockSpec(memory_space=pl.ANY),) * 6,
        scratch_shapes=[pltpu.VMEM((leads * tiles, C), F32), dma((6,))],
        name="write",
    )(*arrays)
    shape = first_kernel.shape
    return (
        pred.reshape(1, leads, rays, gates),
        join[None],
        first.reshape(shape),
        second.reshape(shape),
        gin,
        emb,
    )


def solution(mesh):
    in_specs = (
        P("el", None, None, "az", None),
        P("el"),
        P(),
        P(),
        P(),
        P(),
        P("el", None, None),
        P(),
        P(None, None, "az", None),
    )
    out_specs = (P(None, None, "az", None), P("el", None, None), P(), P(), P(), P())
    return jax.shard_map(shards, mesh=mesh, in_specs=in_specs, out_specs=out_specs, check_vma=False)
```

```python
import functools
import math

import jax
import jax.numpy as jnp
from jax import lax
from jax.experimental import pallas as pl
from jax.experimental.pallas import tpu as pltpu
from jax.sharding import PartitionSpec as P

C = 128
D1 = 1
D2 = 2
HALO = D1 + D2
BF = jnp.bfloat16
F32 = jnp.float32
MESH = pl.DeviceIdType.MESH
NN = (((1,), (0,)), ((), ()))
NT = (((1,), (1,)), ((), ()))
TN = (((0,), (0,)), ((), ()))


def dot(a, b, dims):
    return lax.dot_general(a, b, dims, preferred_element_type=F32)


def up8(n):
    return -(-n // 8) * 8


def up16(n):
    return -(-n // 16) * 16


def logistic(v):
    return 1.0 / (1.0 + jnp.exp(-v))


def slope(v):
    s = logistic(v)
    return s * (1.0 + v * (1.0 - s))


def layouts(sweeps, naz):
    own = C // naz
    share = up8(-(-9 * C // naz))
    chunk = up16(share + own)
    rest = up16(-(-(9 * C + 24 + up8(sweeps)) // naz))
    return (chunk - own, own, chunk), (rest, 0, rest)


def pieces(start, count, share, chunk):
    out = []
    done = 0
    while done < count:
        k, off = divmod(start + done, share)
        size = min(count - done, share - off)
        out.append((done, k * chunk + off, size))
        done += size
    return out


def fill_taps(ref, value, dilate, gates):
    n = value.shape[1]
    gate = lax.broadcasted_iota(jnp.int32, value.shape, 1) % gates
    low = jnp.where(gate >= dilate, pltpu.roll(value, dilate, 1), 0.0)
    high = jnp.where(gate < gates - dilate, pltpu.roll(value, n - dilate, 1), 0.0)
    ref[0:C, :] = low.astype(BF)
    ref[C : 2 * C, :] = value.astype(BF)
    ref[2 * C : 3 * C, :] = high.astype(BF)


def step_kernel(
    parts, naz, nel, gates, rays, scale,
    ids_ref, xc_ref, embed_ref, proj_ref, k1_ref, k2_ref, wj_ref, head_ref,
    pred_out, join_out, first_out, second_out, input_out, embed_out,
    xe, t0, t1, tu2, tu1,
    pack0, pack1, pay0, pay1, abuf0, abuf1, half0, half1,
    rbuf0, rbuf1, mbuf0, mbuf1, gbuf0, gbuf1, pbuf,
    sh, rh, sa, ra, sb, rb, sc, rc, sd, rd, se, re, sp, rp,
):
    packs, pays, abufs, halves = (pack0, pack1), (pay0, pay1), (abuf0, abuf1), (half0, half1)
    rbufs, mbufs, gbufs = (rbuf0, rbuf1), (mbuf0, mbuf1), (gbuf0, gbuf1)
    g = gates
    n = rays * g
    h = HALO * g
    sweeps = embed_ref.shape[0]
    slots = ids_ref.shape[0]
    nq = naz // 2
    a = lax.axis_index("az")
    e = lax.axis_index("el")
    core = lax.rem(a, 2)
    q = a // 2
    started = []

    def at(az, el):
        return {"az": az, "el": el}

    partner = at(a + 1 - 2 * core, e)
    right = at(lax.rem(a + 1, naz), e)
    left = at(lax.rem(a + naz - 1, naz), e)
    same = [at(2 * lax.rem(q + s, nq) + core, e) for s in range(nq)]
    column = [at(a, lax.rem(e + t, nel)) for t in range(nel)]

    barrier = pltpu.get_barrier_semaphore()
    greeted = [partner, right, left] + same[1:] + column[1:]
    for device in greeted:
        pl.semaphore_signal(barrier, inc=1, device_id=device, device_id_type=MESH)
    xe[:, h : h + n] = xc_ref[...]
    pl.semaphore_wait(barrier, len(greeted))

    def send(source, target, ssem, rsem, device):
        c = pltpu.make_async_remote_copy(
            src_ref=source, dst_ref=target, send_sem=ssem, recv_sem=rsem,
            device_id=device, device_id_type=MESH,
        )
        c.start()
        started.append(c)
        return c

    up = send(xc_ref.at[:, n - h : n], xe.at[:, 0:h], sh.at[0], rh.at[0], right)
    down = send(xc_ref.at[:, 0:h], xe.at[:, h + n : n + 2 * h], sh.at[1], rh.at[1], left)

    def rows(index, chunk):
        return pl.ds(pl.multiple_of(index * chunk, 16), chunk)

    def put(i, start, value):
        share, own, chunk = parts[i]
        for src, dst, size in pieces(start, value.shape[0], share, chunk):
            packs[i][dst : dst + size, :] = value[src : src + size, :]

    def phase_a(i):
        chunk = parts[i][2]
        pays[i][...] = packs[i][...].astype(BF)
        return send(
            pays[i].at[rows(1 - core, nq * chunk), :], abufs[i], sa.at[i], ra.at[i], partner
        )

    def phase_b(i, arrived):
        chunk = parts[i][2]
        arrived.wait_recv()
        mine = pays[i][rows(core, nq * chunk), :].astype(F32)
        halves[i][...] = (mine + abufs[i][...].astype(F32)).astype(BF)
        return [
            send(
                halves[i].at[rows(lax.rem(q + s, nq), chunk), :], rbufs[i].at[s],
                sb.at[i, s], rb.at[i, s], same[s],
            )
            for s in range(1, nq)
        ]

    def phase_c(i, arrived):
        chunk = parts[i][2]
        acc = halves[i][rows(q, chunk), :].astype(F32)
        for s in range(1, nq):
            arrived[s - 1].wait_recv()
            acc = acc + rbufs[i][s].astype(F32)
        mbufs[i][e] = acc.astype(BF)
        sent = [
            send(mbufs[i].at[e], mbufs[i].at[e], sc.at[i, t], rc.at[i, t], column[t])
            for t in range(1, nel)
        ]
        return acc, sent

    def phase_d(i, acc, arrived):
        share, own, chunk = parts[i]
        for c in arrived:
            c.wait_recv()
        total = mbufs[i][0].astype(F32)
        for t in range(1, nel):
            total = total + mbufs[i][t].astype(F32)
        if own:
            line = lax.broadcasted_iota(jnp.int32, total.shape, 0)
            total = jnp.where(line < share, total, acc)
        mine = rows(core * nq + q, chunk)
        gbufs[i][mine, :] = total.astype(BF)
        view = gbufs[i].at[mine, :]
        sent = [send(view, view, sd.at[i, s], rd.at[i, s], same[s]) for s in range(1, nq)]
        own_sent = send(view, view, se.at[i, 0], re.at[i, 0], partner)
        return sent, own_sent

    def phase_e(i, arrived, own_sent):
        chunk = parts[i][2]
        last = [own_sent]
        for s in range(1, nq):
            arrived[s - 1].wait_recv()
            view = gbufs[i].at[rows(core * nq + lax.rem(q + nq - s, nq), chunk), :]
            last.append(send(view, view, se.at[i, s], re.at[i, s], partner))
        return last

    def take(i, ref, start):
        share, own, chunk = parts[i]
        for dst, src, size in pieces(start, ref.shape[0], share, chunk):
            ref[dst : dst + size, :] = gbufs[i][src : src + size, :].astype(F32)

    def conv(k_ref, taps, first, step, width):
        total = None
        for p in range(3):
            kp = k_ref[p * 3 * C : (p + 1) * 3 * C, :]
            term = dot(kp, taps[:, first + p * step : first + p * step + width], TN)
            total = term if total is None else total + term
        return total

    def back(k_ref, taps, step, width):
        total = None
        for p in range(3):
            m = jnp.concatenate(
                [
                    k_ref[((2 - p) * 3 + 2 - q_) * C : ((2 - p) * 3 + 3 - q_) * C, :]
                    for q_ in range(3)
                ],
                axis=1,
            )
            term = dot(m, taps[:, p * step : p * step + width], NN)
            total = term if total is None else total + term
        return total

    packs[0][...] = jnp.zeros_like(packs[0])
    packs[1][...] = jnp.zeros_like(packs[1])
    owns = []
    row = jnp.zeros((1, C), F32)
    for s in range(sweeps):
        w = jnp.float32(0.0)
        for j in range(slots):
            w = w + jnp.where(ids_ref[j] == s, 1.0, 0.0)
        owns.append(w)
        row = row + w * embed_ref[s : s + 1, :]
    bias = jnp.broadcast_to(row, (C, C)).T[:, 0:1]

    up.wait_recv()
    down.wait_recv()
    proj = proj_ref[...].astype(F32)
    proj = jnp.concatenate([proj] * slots, axis=0).astype(BF)
    s0 = (dot(proj, xe[0:48, :], TN) + bias).astype(BF).astype(F32)
    fill_taps(t0, s0 * logistic(s0), D1, g)

    w1 = (rays + 2 * D2) * g
    s1 = s0[:, D1 * g : D1 * g + w1] + conv(k1_ref, t0, 0, D1 * g, w1)
    s1 = s1.astype(BF).astype(F32)
    fill_taps(t1, s1 * logistic(s1), D2, g)
    s2 = s1[:, D2 * g : D2 * g + n] + conv(k2_ref, t1, 0, D2 * g, n)
    s2 = s2.astype(BF)

    jb = dot(head_ref[...], xe[48:60, :], TN).astype(BF)
    join = dot(s2, jb[:, HALO * g : HALO * g + n], NT) * scale
    share, own, chunk = parts[0]
    for k in range(naz):
        packs[0][k * chunk + share : (k + 1) * chunk, :] = join[k * own : (k + 1) * own, :]

    g2 = dot(wj_ref[...], jb, NN)
    fill_taps(tu2, g2, D2, g)
    for p in range(3):
        part = dot(
            t1[:, p * D2 * g : p * D2 * g + n], tu2[C : 2 * C, HALO * g : HALO * g + n], NT
        )
        put(0, p * 3 * C, part * scale)
    a0 = phase_a(0)

    joined = dot(wj_ref[...], s2, TN).astype(BF)
    pbuf[e] = dot(head_ref[...], joined, NN)

    wb = (rays + 2 * D1) * g
    g1 = g2[:, D2 * g : D2 * g + wb] + back(k2_ref, tu2, D2 * g, wb) * slope(
        s1[:, (D2 - D1) * g : (D2 - D1) * g + wb]
    )
    b0 = phase_b(0, a0)
    fill_taps(tu1, g1, D1, g)
    for p in range(3):
        first = (HALO + D1 * (p - 1)) * g
        part = dot(t0[:, first : first + n], tu1[C : 2 * C, D1 * g : D1 * g + n], NT)
        put(1, p * 3 * C, part * scale)
    g0 = g1[:, D1 * g : D1 * g + n] + back(k1_ref, tu1, D1 * g, n) * slope(
        s0[:, HALO * g : HALO * g + n]
    )
    g0 = g0.astype(BF)
    gin = dot(xe[0:48, HALO * g : HALO * g + n], g0, NT)
    put(1, 9 * C, (gin[0:24, :] + gin[24:48, :]) * scale)
    summed = dot(jnp.ones((8, n), BF), g0, NT)[0:1, :] * scale
    lines = up8(sweeps)
    index = lax.broadcasted_iota(jnp.int32, (lines, C), 0)
    grads = jnp.zeros((lines, C), F32)
    for s in range(sweeps):
        grads = grads + jnp.where(index == s, owns[s] * summed, 0.0)
    put(1, 9 * C + 24, grads)
    a1 = phase_a(1)
    acc0, c0 = phase_c(0, b0)
    b1 = phase_b(1, a1)
    d0, own0 = phase_d(0, acc0, c0)
    preds = [
        send(pbuf.at[e], pbuf.at[e], sp.at[t], rp.at[t], column[t]) for t in range(1, nel)
    ]
    acc1, c1 = phase_c(1, b1)
    d1, own1 = phase_d(1, acc1, c1)
    e0 = phase_e(0, d0, own0)
    for c in preds:
        c.wait_recv()
    pred = pbuf[0]
    for t in range(1, nel):
        pred = pred + pbuf[t]
    pred_out[...] = pred
    for c in e0:
        c.wait_recv()
    take(0, second_out, 0)
    for k in range(naz):
        join_out[k * own : (k + 1) * own, :] = gbufs[0][
            k * chunk + share : (k + 1) * chunk, :
        ].astype(F32)
    e1 = phase_e(1, d1, own1)
    for c in e1:
        c.wait_recv()
    take(1, first_out, 0)
    take(1, input_out, 9 * C)
    take(1, embed_out, 9 * C + 24)
    for c in started:
        c.wait_send()


def write_kernel(*refs):
    ins, outs, (lines, sems) = refs[0:6], refs[6:12], refs[12:14]
    copies = [pltpu.make_async_copy(ins[i], outs[i], sems.at[i]) for i in range(1, 6)]
    for c in copies:
        c.start()
    leads, n = ins[0].shape
    tiles = n // C
    for t in range(tiles):
        lines[pl.ds(t, leads, stride=tiles), :] = ins[0][:, t * C : (t + 1) * C]
    last = pltpu.make_async_copy(lines, outs[0], sems.at[0])
    last.start()
    for c in copies:
        c.wait()
    last.wait()


def shards(
    raw_sweeps, sweep_ids, elevation_embed, input_proj, first_kernel, second_kernel,
    join_weight, head_weight, cotangent,
):
    naz = lax.axis_size("az")
    nel = lax.axis_size("el")
    slots, _, inputs, rays, gates = raw_sweeps.shape
    leads = head_weight.shape[0]
    sweeps = elevation_embed.shape[0]
    parts = layouts(sweeps, naz)
    scale = 1.0 / math.sqrt(nel * rays * naz * gates)
    n = rays * gates
    h = HALO * gates
    nq = naz // 2

    xc = jnp.concatenate(
        [
            raw_sweeps.reshape(slots * inputs, n),
            cotangent.reshape(leads, n),
        ],
        axis=0,
    )
    vm = pl.BlockSpec(memory_space=pltpu.VMEM)
    dma = pltpu.SemaphoreType.DMA

    def both(shape, kind=BF):
        return [pltpu.VMEM(shape(chunk), kind) for _, _, chunk in parts]

    pred, join, first, second, gin, emb = pl.pallas_call(
        functools.partial(step_kernel, parts, naz, nel, gates, rays, scale),
        out_shape=(
            jax.ShapeDtypeStruct((leads, n), F32),
            jax.ShapeDtypeStruct((C, C), F32),
            jax.ShapeDtypeStruct((9 * C, C), F32),
            jax.ShapeDtypeStruct((9 * C, C), F32),
            jax.ShapeDtypeStruct((inputs, C), F32),
            jax.ShapeDtypeStruct((sweeps, C), F32),
        ),
        in_specs=[pl.BlockSpec(memory_space=pltpu.SMEM)] + [vm] * 7,
        out_specs=(vm,) * 6,
        scratch_shapes=[
            pltpu.VMEM((60, n + 2 * h), BF),
            pltpu.VMEM((3 * C, n + 2 * h), BF),
            pltpu.VMEM((3 * C, (rays + 2 * D2) * gates), BF),
            pltpu.VMEM((3 * C, n + 2 * h), BF),
            pltpu.VMEM((3 * C, (rays + 2 * D1) * gates), BF),
        ]
        + both(lambda chunk: (naz * chunk, C), F32)
        + both(lambda chunk: (naz * chunk, C))
        + both(lambda chunk: (nq * chunk, C))
        + both(lambda chunk: (nq * chunk, C))
        + both(lambda chunk: (nq, chunk, C))
        + both(lambda chunk: (nel, chunk, C))
        + both(lambda chunk: (naz * chunk, C))
        + [
            pltpu.VMEM((nel, leads, n), F32),
            dma((2,)), dma((2,)),
            dma((2,)), dma((2,)),
            dma((2, nq)), dma((2, nq)),
            dma((2, nel)), dma((2, nel)),
            dma((2, nq)), dma((2, nq)),
            dma((2, nq)), dma((2, nq)),
            dma((nel,)), dma((nel,)),
        ],
        compiler_params=pltpu.CompilerParams(
            collective_id=0, has_side_effects=True, vmem_limit_bytes=48 * 1024 * 1024
        ),
        name="step",
    )(
        sweep_ids, xc, elevation_embed, input_proj,
        first_kernel.reshape(9 * C, C), second_kernel.reshape(9 * C, C),
        join_weight[0], head_weight,
    )
    tiles = n // C
    arrays = (pred, join, first, second, gin, emb)
    kinds = [jax.ShapeDtypeStruct((leads * tiles, C), F32)]
    kinds += [jax.ShapeDtypeStruct(v.shape, F32) for v in arrays[1:]]
    pred, join, first, second, gin, emb = pl.pallas_call(
        write_kernel,
        out_shape=tuple(kinds),
        in_specs=[vm] * 6,
        out_specs=(pl.BlockSpec(memory_space=pl.ANY),) * 6,
        scratch_shapes=[pltpu.VMEM((leads * tiles, C), F32), dma((6,))],
        compiler_params=pltpu.CompilerParams(vmem_limit_bytes=4 * 1024 * 1024),
        name="write",
    )(*arrays)
    shape = first_kernel.shape
    return (
        pred.reshape(1, leads, rays, gates),
        join[None],
        first.reshape(shape),
        second.reshape(shape),
        gin,
        emb,
    )


def solution(mesh):
    in_specs = (
        P("el", None, None, "az", None),
        P("el"),
        P(),
        P(),
        P(),
        P(),
        P("el", None, None),
        P(),
        P(None, None, "az", None),
    )
    out_specs = (P(None, None, "az", None), P("el", None, None), P(), P(), P(), P())
    return jax.shard_map(shards, mesh=mesh, in_specs=in_specs, out_specs=out_specs, check_vma=False)
```

```python
import functools
import math

import jax
import jax.numpy as jnp
from jax import lax
from jax.experimental import pallas as pl
from jax.experimental.pallas import tpu as pltpu
from jax.sharding import PartitionSpec as P

C = 128
D1 = 1
D2 = 2
HALO = D1 + D2
BF = jnp.bfloat16
F32 = jnp.float32
MESH = pl.DeviceIdType.MESH
NN = (((1,), (0,)), ((), ()))
NT = (((1,), (1,)), ((), ()))
TN = (((0,), (0,)), ((), ()))


def dot(a, b, dims):
    return lax.dot_general(a, b, dims, preferred_element_type=F32)


def up8(n):
    return -(-n // 8) * 8


def up16(n):
    return -(-n // 16) * 16


def logistic(v):
    return 1.0 / (1.0 + jnp.exp(-v))


def slope(v):
    s = logistic(v)
    return s * (1.0 + v * (1.0 - s))


def layouts(sweeps, naz, nel):
    count = naz * nel
    own = C // naz
    chunk = up16(up8(-(-9 * C // count)) + own)
    rest = up16(-(-(9 * C + 24 + up8(sweeps)) // count))
    return (chunk - own, own, chunk), (rest, 0, rest)


def pieces(start, count, share, chunk):
    out = []
    done = 0
    while done < count:
        k, off = divmod(start + done, share)
        size = min(count - done, share - off)
        out.append((done, k * chunk + off, size))
        done += size
    return out


def fill_taps(ref, value, dilate, gates):
    n = value.shape[1]
    gate = lax.broadcasted_iota(jnp.int32, value.shape, 1) % gates
    low = jnp.where(gate >= dilate, pltpu.roll(value, dilate, 1), 0.0)
    high = jnp.where(gate < gates - dilate, pltpu.roll(value, n - dilate, 1), 0.0)
    ref[0:C, :] = low.astype(BF)
    ref[C : 2 * C, :] = value.astype(BF)
    ref[2 * C : 3 * C, :] = high.astype(BF)


def step_kernel(
    parts, naz, nel, gates, rays, scale,
    ids_ref, xc_ref, embed_ref, proj_ref, k1_ref, k2_ref, wj_ref, head_ref,
    pred_out, join_out, first_out, second_out, input_out, embed_out,
    xe, t0, t1, tu2, tu1,
    pack0, pack1, pay0, pay1, abuf0, abuf1, half0, half1,
    block0, block1, ybuf0, ybuf1, rbuf0, rbuf1, gbuf0, gbuf1, pbuf,
    sh, rh, sa, ra, sb, rb, sc, rc, sd, rd, sy, ry, se, re, sp, rp,
):
    packs, pays, abufs, halves = (pack0, pack1), (pay0, pay1), (abuf0, abuf1), (half0, half1)
    rbufs, ybufs, gbufs = (rbuf0, rbuf1), (ybuf0, ybuf1), (gbuf0, gbuf1)
    blocks = (block0, block1)
    g = gates
    n = rays * g
    h = HALO * g
    sweeps = embed_ref.shape[0]
    slots = ids_ref.shape[0]
    nq = naz // 2
    a = lax.axis_index("az")
    e = lax.axis_index("el")
    core = lax.rem(a, 2)
    q = a // 2
    started = []

    def at(az, el):
        return {"az": az, "el": el}

    partner = at(a + 1 - 2 * core, e)
    right = at(lax.rem(a + 1, naz), e)
    left = at(lax.rem(a + naz - 1, naz), e)
    same = [at(2 * lax.rem(q + s, nq) + core, e) for s in range(nq)]
    column = [at(a, lax.rem(e + t, nel)) for t in range(nel)]

    barrier = pltpu.get_barrier_semaphore()
    greeted = [partner, right, left] + same[1:] + column[1:]
    for device in greeted:
        pl.semaphore_signal(barrier, inc=1, device_id=device, device_id_type=MESH)
    xe[:, h : h + n] = xc_ref[...]
    pl.semaphore_wait(barrier, len(greeted))

    def send(source, target, ssem, rsem, device):
        c = pltpu.make_async_remote_copy(
            src_ref=source, dst_ref=target, send_sem=ssem, recv_sem=rsem,
            device_id=device, device_id_type=MESH,
        )
        c.start()
        started.append(c)
        return c

    up = send(xc_ref.at[:, n - h : n], xe.at[:, 0:h], sh.at[0], rh.at[0], right)
    down = send(xc_ref.at[:, 0:h], xe.at[:, h + n : n + 2 * h], sh.at[1], rh.at[1], left)

    def rows(index, chunk):
        return pl.ds(pl.multiple_of(index * chunk, 16), chunk)

    def put(i, start, value):
        share, own, chunk = parts[i]
        for src, dst, size in pieces(start, value.shape[0], share, chunk):
            packs[i][dst : dst + size, :] = value[src : src + size, :]

    def place(c_, e_, q_):
        return (c_ * nel + e_) * nq + q_

    def phase_a(i):
        size = nel * nq * parts[i][2]
        pays[i][...] = packs[i][...].astype(BF)
        return send(
            pays[i].at[rows(1 - core, size), :], abufs[i], sa.at[i], ra.at[i], partner
        )

    def phase_y(i, arrived):
        chunk = parts[i][2]
        arrived.wait_recv()
        mine = pays[i][rows(core, nel * nq * chunk), :].astype(F32)
        halves[i][...] = (mine + abufs[i][...].astype(F32)).astype(BF)
        return [
            send(
                halves[i].at[rows(lax.rem(e + t, nel), nq * chunk), :], ybufs[i].at[t],
                sc.at[i, t], rc.at[i, t], column[t],
            )
            for t in range(1, nel)
        ]

    def phase_b(i, arrived):
        chunk = parts[i][2]
        total = halves[i][rows(e, nq * chunk), :].astype(F32)
        for t in range(1, nel):
            arrived[t - 1].wait_recv()
            total = total + ybufs[i][t].astype(F32)
        blocks[i][...] = total.astype(BF)
        return [
            send(
                blocks[i].at[rows(lax.rem(q + s, nq), chunk), :], rbufs[i].at[s],
                sb.at[i, s], rb.at[i, s], same[s],
            )
            for s in range(1, nq)
        ]

    def share_line(i, s, view):
        return [
            send(view, view, sy.at[i, s, t], ry.at[i, s, t], column[t]) for t in range(1, nel)
        ]

    def phase_d(i, arrived):
        chunk = parts[i][2]
        total = blocks[i][rows(q, chunk), :].astype(F32)
        for s in range(1, nq):
            arrived[s - 1].wait_recv()
            total = total + rbufs[i][s].astype(F32)
        mine = rows(place(core, e, q), chunk)
        gbufs[i][mine, :] = total.astype(BF)
        view = gbufs[i].at[mine, :]
        sent = [send(view, view, sd.at[i, s], rd.at[i, s], same[s]) for s in range(1, nq)]
        return sent, share_line(i, 0, view)

    def phase_e(i, arrived, lines):
        chunk = parts[i][2]
        for s in range(1, nq):
            arrived[s - 1].wait_recv()
            m = place(core, e, lax.rem(q + nq - s, nq))
            lines = lines + share_line(i, s, gbufs[i].at[rows(m, chunk), :])
        view = gbufs[i].at[rows(core * nel + e, nq * chunk), :]
        return lines, send(view, view, se.at[i, 0], re.at[i, 0], partner)

    def phase_f(i, lines, last):
        size = nq * parts[i][2]
        last = [last]
        for c in lines:
            c.wait_recv()
        for t in range(1, nel):
            view = gbufs[i].at[rows(core * nel + lax.rem(e + nel - t, nel), size), :]
            last.append(send(view, view, se.at[i, t], re.at[i, t], partner))
        return last

    def take(i, ref, start):
        share, own, chunk = parts[i]
        for dst, src, size in pieces(start, ref.shape[0], share, chunk):
            ref[dst : dst + size, :] = gbufs[i][src : src + size, :].astype(F32)

    def conv(k_ref, taps, first, step, width):
        total = None
        for p in range(3):
            kp = k_ref[p * 3 * C : (p + 1) * 3 * C, :]
            term = dot(kp, taps[:, first + p * step : first + p * step + width], TN)
            total = term if total is None else total + term
        return total

    def back(k_ref, taps, step, width):
        total = None
        for p in range(3):
            m = jnp.concatenate(
                [
                    k_ref[((2 - p) * 3 + 2 - q_) * C : ((2 - p) * 3 + 3 - q_) * C, :]
                    for q_ in range(3)
                ],
                axis=1,
            )
            term = dot(m, taps[:, p * step : p * step + width], NN)
            total = term if total is None else total + term
        return total

    packs[0][...] = jnp.zeros_like(packs[0])
    packs[1][...] = jnp.zeros_like(packs[1])
    owns = []
    row = jnp.zeros((1, C), F32)
    for s in range(sweeps):
        w = jnp.float32(0.0)
        for j in range(slots):
            w = w + jnp.where(ids_ref[j] == s, 1.0, 0.0)
        owns.append(w)
        row = row + w * embed_ref[s : s + 1, :]
    bias = jnp.broadcast_to(row, (C, C)).T[:, 0:1]

    up.wait_recv()
    down.wait_recv()
    proj = proj_ref[...].astype(F32)
    proj = jnp.concatenate([proj] * slots, axis=0).astype(BF)
    s0 = (dot(proj, xe[0:48, :], TN) + bias).astype(BF).astype(F32)
    fill_taps(t0, s0 * logistic(s0), D1, g)

    w1 = (rays + 2 * D2) * g
    s1 = s0[:, D1 * g : D1 * g + w1] + conv(k1_ref, t0, 0, D1 * g, w1)
    s1 = s1.astype(BF).astype(F32)
    fill_taps(t1, s1 * logistic(s1), D2, g)
    s2 = s1[:, D2 * g : D2 * g + n] + conv(k2_ref, t1, 0, D2 * g, n)
    s2 = s2.astype(BF)

    jb = dot(head_ref[...], xe[48:60, :], TN).astype(BF)
    join = dot(s2, jb[:, HALO * g : HALO * g + n], NT) * scale
    share, own, chunk = parts[0]
    for k in range(naz):
        first = pl.multiple_of(place(k // nq, e, k % nq) * chunk + share, 8)
        packs[0][pl.ds(first, own), :] = join[k * own : (k + 1) * own, :]

    g2 = dot(wj_ref[...], jb, NN)
    fill_taps(tu2, g2, D2, g)
    for p in range(3):
        part = dot(
            t1[:, p * D2 * g : p * D2 * g + n], tu2[C : 2 * C, HALO * g : HALO * g + n], NT
        )
        put(0, p * 3 * C, part * scale)
    a0 = phase_a(0)

    joined = dot(wj_ref[...], s2, TN).astype(BF)
    pbuf[e] = dot(head_ref[...], joined, NN)

    wb = (rays + 2 * D1) * g
    g1 = g2[:, D2 * g : D2 * g + wb] + back(k2_ref, tu2, D2 * g, wb) * slope(
        s1[:, (D2 - D1) * g : (D2 - D1) * g + wb]
    )
    y0 = phase_y(0, a0)
    fill_taps(tu1, g1, D1, g)
    for p in range(3):
        first = (HALO + D1 * (p - 1)) * g
        part = dot(t0[:, first : first + n], tu1[C : 2 * C, D1 * g : D1 * g + n], NT)
        put(1, p * 3 * C, part * scale)
    b0 = phase_b(0, y0)
    g0 = g1[:, D1 * g : D1 * g + n] + back(k1_ref, tu1, D1 * g, n) * slope(
        s0[:, HALO * g : HALO * g + n]
    )
    g0 = g0.astype(BF)
    gin = dot(xe[0:48, HALO * g : HALO * g + n], g0, NT)
    put(1, 9 * C, (gin[0:24, :] + gin[24:48, :]) * scale)
    summed = dot(jnp.ones((8, n), BF), g0, NT)[0:1, :] * scale
    lines = up8(sweeps)
    index = lax.broadcasted_iota(jnp.int32, (lines, C), 0)
    grads = jnp.zeros((lines, C), F32)
    for s in range(sweeps):
        grads = grads + jnp.where(index == s, owns[s] * summed, 0.0)
    put(1, 9 * C + 24, grads)
    a1 = phase_a(1)
    d0, l0 = phase_d(0, b0)
    y1 = phase_y(1, a1)
    preds = [
        send(pbuf.at[e], pbuf.at[e], sp.at[t], rp.at[t], column[t]) for t in range(1, nel)
    ]
    b1 = phase_b(1, y1)
    l0, e0 = phase_e(0, d0, l0)
    d1, l1 = phase_d(1, b1)
    f0 = phase_f(0, l0, e0)
    for c in preds:
        c.wait_recv()
    pred = pbuf[0]
    for t in range(1, nel):
        pred = pred + pbuf[t]
    pred_out[...] = pred
    for c in f0:
        c.wait_recv()
    take(0, second_out, 0)
    for k in range(naz):
        line = gbufs[0][rows(place(k // nq, e, k % nq), chunk), :].astype(F32)
        join_out[k * own : (k + 1) * own, :] = line[share : share + own, :]
    l1, e1 = phase_e(1, d1, l1)
    f1 = phase_f(1, l1, e1)
    for c in f1:
        c.wait_recv()
    take(1, first_out, 0)
    take(1, input_out, 9 * C)
    take(1, embed_out, 9 * C + 24)
    for c in started:
        c.wait_send()


def write_kernel(*refs):
    ins, outs, (lines, sems) = refs[0:6], refs[6:12], refs[12:14]
    copies = [pltpu.make_async_copy(ins[i], outs[i], sems.at[i]) for i in range(1, 6)]
    for c in copies:
        c.start()
    leads, n = ins[0].shape
    tiles = n // C
    for t in range(tiles):
        lines[pl.ds(t, leads, stride=tiles), :] = ins[0][:, t * C : (t + 1) * C]
    last = pltpu.make_async_copy(lines, outs[0], sems.at[0])
    last.start()
    for c in copies:
        c.wait()
    last.wait()


def shards(
    raw_sweeps, sweep_ids, elevation_embed, input_proj, first_kernel, second_kernel,
    join_weight, head_weight, cotangent,
):
    naz = lax.axis_size("az")
    nel = lax.axis_size("el")
    slots, _, inputs, rays, gates = raw_sweeps.shape
    leads = head_weight.shape[0]
    sweeps = elevation_embed.shape[0]
    parts = layouts(sweeps, naz, nel)
    scale = 1.0 / math.sqrt(nel * rays * naz * gates)
    n = rays * gates
    h = HALO * gates
    nq = naz // 2

    xc = jnp.concatenate(
        [
            raw_sweeps.reshape(slots * inputs, n),
            cotangent.reshape(leads, n),
        ],
        axis=0,
    )
    vm = pl.BlockSpec(memory_space=pltpu.VMEM)
    dma = pltpu.SemaphoreType.DMA

    def both(shape, kind=BF):
        return [pltpu.VMEM(shape(chunk), kind) for _, _, chunk in parts]

    pred, join, first, second, gin, emb = pl.pallas_call(
        functools.partial(step_kernel, parts, naz, nel, gates, rays, scale),
        out_shape=(
            jax.ShapeDtypeStruct((leads, n), F32),
            jax.ShapeDtypeStruct((C, C), F32),
            jax.ShapeDtypeStruct((9 * C, C), F32),
            jax.ShapeDtypeStruct((9 * C, C), F32),
            jax.ShapeDtypeStruct((inputs, C), F32),
            jax.ShapeDtypeStruct((sweeps, C), F32),
        ),
        in_specs=[pl.BlockSpec(memory_space=pltpu.SMEM)] + [vm] * 7,
        out_specs=(vm,) * 6,
        scratch_shapes=[
            pltpu.VMEM((60, n + 2 * h), BF),
            pltpu.VMEM((3 * C, n + 2 * h), BF),
            pltpu.VMEM((3 * C, (rays + 2 * D2) * gates), BF),
            pltpu.VMEM((3 * C, n + 2 * h), BF),
            pltpu.VMEM((3 * C, (rays + 2 * D1) * gates), BF),
        ]
        + both(lambda chunk: (naz * nel * chunk, C), F32)
        + both(lambda chunk: (naz * nel * chunk, C))
        + both(lambda chunk: (nq * nel * chunk, C))
        + both(lambda chunk: (nq * nel * chunk, C))
        + both(lambda chunk: (nq * chunk, C))
        + both(lambda chunk: (nel, nq * chunk, C))
        + both(lambda chunk: (nq, chunk, C))
        + both(lambda chunk: (naz * nel * chunk, C))
        + [
            pltpu.VMEM((nel, leads, n), F32),
            dma((2,)), dma((2,)),
            dma((2,)), dma((2,)),
            dma((2, nq)), dma((2, nq)),
            dma((2, nel)), dma((2, nel)),
            dma((2, nq)), dma((2, nq)),
            dma((2, nq, nel)), dma((2, nq, nel)),
            dma((2, nel)), dma((2, nel)),
            dma((nel,)), dma((nel,)),
        ],
        compiler_params=pltpu.CompilerParams(
            collective_id=0, has_side_effects=True, vmem_limit_bytes=48 * 1024 * 1024
        ),
        name="step",
    )(
        sweep_ids, xc, elevation_embed, input_proj,
        first_kernel.reshape(9 * C, C), second_kernel.reshape(9 * C, C),
        join_weight[0], head_weight,
    )
    tiles = n // C
    arrays = (pred, join, first, second, gin, emb)
    kinds = [jax.ShapeDtypeStruct((leads * tiles, C), F32)]
    kinds += [jax.ShapeDtypeStruct(v.shape, F32) for v in arrays[1:]]
    pred, join, first, second, gin, emb = pl.pallas_call(
        write_kernel,
        out_shape=tuple(kinds),
        in_specs=[vm] * 6,
        out_specs=(pl.BlockSpec(memory_space=pl.ANY),) * 6,
        scratch_shapes=[pltpu.VMEM((leads * tiles, C), F32), dma((6,))],
        compiler_params=pltpu.CompilerParams(vmem_limit_bytes=4 * 1024 * 1024),
        name="write",
    )(*arrays)
    shape = first_kernel.shape
    return (
        pred.reshape(1, leads, rays, gates),
        join[None],
        first.reshape(shape),
        second.reshape(shape),
        gin,
        emb,
    )


def solution(mesh):
    in_specs = (
        P("el", None, None, "az", None),
        P("el"),
        P(),
        P(),
        P(),
        P(),
        P("el", None, None),
        P(),
        P(None, None, "az", None),
    )
    out_specs = (P(None, None, "az", None), P("el", None, None), P(), P(), P(), P())
    return jax.shard_map(shards, mesh=mesh, in_specs=in_specs, out_specs=out_specs, check_vma=False)
```

```python
import functools
import math

import jax
import jax.numpy as jnp
from jax import lax
from jax.experimental import pallas as pl
from jax.experimental.pallas import tpu as pltpu
from jax.sharding import PartitionSpec as P

C = 128
D1 = 1
D2 = 2
HALO = D1 + D2
BF = jnp.bfloat16
F32 = jnp.float32
MESH = pl.DeviceIdType.MESH
NN = (((1,), (0,)), ((), ()))
NT = (((1,), (1,)), ((), ()))
TN = (((0,), (0,)), ((), ()))


def dot(a, b, dims):
    return lax.dot_general(a, b, dims, preferred_element_type=F32)


def up8(n):
    return -(-n // 8) * 8


def up16(n):
    return -(-n // 16) * 16


def logistic(v):
    return 1.0 / (1.0 + jnp.exp(-v))


def slope(v):
    s = logistic(v)
    return s * (1.0 + v * (1.0 - s))


def layouts(sweeps, naz):
    own = C // naz
    share = up8(-(-9 * C // naz))
    chunk = up16(share + own)
    rest = up16(-(-(9 * C + 24 + up8(sweeps)) // naz))
    return (chunk - own, own, chunk), (rest, 0, rest)


def pieces(start, count, share, chunk):
    out = []
    done = 0
    while done < count:
        k, off = divmod(start + done, share)
        size = min(count - done, share - off)
        out.append((done, k * chunk + off, size))
        done += size
    return out


def fill_taps(ref, value, dilate, gates):
    n = value.shape[1]
    gate = lax.broadcasted_iota(jnp.int32, value.shape, 1) % gates
    low = jnp.where(gate >= dilate, pltpu.roll(value, dilate, 1), 0.0)
    high = jnp.where(gate < gates - dilate, pltpu.roll(value, n - dilate, 1), 0.0)
    ref[0:C, :] = low.astype(BF)
    ref[C : 2 * C, :] = value.astype(BF)
    ref[2 * C : 3 * C, :] = high.astype(BF)


def step_kernel(
    parts, naz, nel, gates, rays, scale,
    ids_ref, xc_ref, embed_ref, proj_ref, k1_ref, k2_ref, wj_ref, head_ref,
    pred_out, join_out, first_out, second_out, input_out, embed_out,
    xe, t0, t1, tu2, tu1,
    pack0, pack1, pay0, pay1, abuf0, abuf1, half0, half1,
    rbuf0, rbuf1, mbuf0, mbuf1, gbuf0, gbuf1, pbuf,
    sh, rh, sa, ra, sb, rb, sc, rc, sd, rd, se, re, sp, rp,
):
    packs, pays, abufs, halves = (pack0, pack1), (pay0, pay1), (abuf0, abuf1), (half0, half1)
    rbufs, mbufs, gbufs = (rbuf0, rbuf1), (mbuf0, mbuf1), (gbuf0, gbuf1)
    g = gates
    n = rays * g
    h = HALO * g
    sweeps = embed_ref.shape[0]
    slots = ids_ref.shape[0]
    nq = naz // 2
    a = lax.axis_index("az")
    e = lax.axis_index("el")
    core = lax.rem(a, 2)
    q = a // 2
    started = []

    def at(az, el):
        return {"az": az, "el": el}

    partner = at(a + 1 - 2 * core, e)
    right = at(lax.rem(a + 1, naz), e)
    left = at(lax.rem(a + naz - 1, naz), e)
    same = [at(2 * lax.rem(q + s, nq) + core, e) for s in range(nq)]
    column = [at(a, lax.rem(e + t, nel)) for t in range(nel)]

    barrier = pltpu.get_barrier_semaphore()
    greeted = [partner, right, left] + same[1:] + column[1:]
    for device in greeted:
        pl.semaphore_signal(barrier, inc=1, device_id=device, device_id_type=MESH)
    xe[:, h : h + n] = xc_ref[...]
    pl.semaphore_wait(barrier, len(greeted))

    def send(source, target, ssem, rsem, device):
        c = pltpu.make_async_remote_copy(
            src_ref=source, dst_ref=target, send_sem=ssem, recv_sem=rsem,
            device_id=device, device_id_type=MESH,
        )
        c.start()
        started.append(c)
        return c

    up = send(xc_ref.at[:, n - h : n], xe.at[:, 0:h], sh.at[0], rh.at[0], right)
    down = send(xc_ref.at[:, 0:h], xe.at[:, h + n : n + 2 * h], sh.at[1], rh.at[1], left)

    def rows(index, chunk):
        return pl.ds(pl.multiple_of(index * chunk, 16), chunk)

    def put(i, start, value):
        share, own, chunk = parts[i]
        for src, dst, size in pieces(start, value.shape[0], share, chunk):
            packs[i][dst : dst + size, :] = value[src : src + size, :]

    def phase_a(i):
        chunk = parts[i][2]
        pays[i][...] = packs[i][...].astype(BF)
        return send(
            pays[i].at[rows(1 - core, nq * chunk), :], abufs[i], sa.at[i], ra.at[i], partner
        )

    def phase_b(i, arrived):
        chunk = parts[i][2]
        arrived.wait_recv()
        mine = pays[i][rows(core, nq * chunk), :].astype(F32)
        halves[i][...] = (mine + abufs[i][...].astype(F32)).astype(BF)
        return [
            send(
                halves[i].at[rows(lax.rem(q + s, nq), chunk), :], rbufs[i].at[s],
                sb.at[i, s], rb.at[i, s], same[s],
            )
            for s in range(1, nq)
        ]

    def phase_c(i, arrived):
        chunk = parts[i][2]
        acc = halves[i][rows(q, chunk), :].astype(F32)
        for s in range(1, nq):
            arrived[s - 1].wait_recv()
            acc = acc + rbufs[i][s].astype(F32)
        mbufs[i][e] = acc.astype(BF)
        sent = [
            send(mbufs[i].at[e], mbufs[i].at[e], sc.at[i, t], rc.at[i, t], column[t])
            for t in range(1, nel)
        ]
        return acc, sent

    def phase_d(i, acc, arrived):
        share, own, chunk = parts[i]
        for c in arrived:
            c.wait_recv()
        total = mbufs[i][0].astype(F32)
        for t in range(1, nel):
            total = total + mbufs[i][t].astype(F32)
        if own:
            line = lax.broadcasted_iota(jnp.int32, total.shape, 0)
            total = jnp.where(line < share, total, acc)
        mine = rows(core * nq + q, chunk)
        gbufs[i][mine, :] = total.astype(BF)
        view = gbufs[i].at[mine, :]
        sent = [send(view, view, sd.at[i, s], rd.at[i, s], same[s]) for s in range(1, nq)]
        return sent

    def phase_e(i, arrived):
        for c in arrived:
            c.wait_recv()
        view = gbufs[i].at[rows(core, nq * parts[i][2]), :]
        return [send(view, view, se.at[i, 0], re.at[i, 0], partner)]

    def take(i, ref, start):
        share, own, chunk = parts[i]
        for dst, src, size in pieces(start, ref.shape[0], share, chunk):
            ref[dst : dst + size, :] = gbufs[i][src : src + size, :].astype(F32)

    def conv(k_ref, taps, first, step, width):
        total = None
        for p in range(3):
            kp = k_ref[p * 3 * C : (p + 1) * 3 * C, :]
            term = dot(kp, taps[:, first + p * step : first + p * step + width], TN)
            total = term if total is None else total + term
        return total

    def back(k_ref, taps, step, width):
        total = None
        for p in range(3):
            m = jnp.concatenate(
                [
                    k_ref[((2 - p) * 3 + 2 - q_) * C : ((2 - p) * 3 + 3 - q_) * C, :]
                    for q_ in range(3)
                ],
                axis=1,
            )
            term = dot(m, taps[:, p * step : p * step + width], NN)
            total = term if total is None else total + term
        return total

    packs[0][...] = jnp.zeros_like(packs[0])
    packs[1][...] = jnp.zeros_like(packs[1])
    owns = []
    row = jnp.zeros((1, C), F32)
    for s in range(sweeps):
        w = jnp.float32(0.0)
        for j in range(slots):
            w = w + jnp.where(ids_ref[j] == s, 1.0, 0.0)
        owns.append(w)
        row = row + w * embed_ref[s : s + 1, :]
    bias = jnp.broadcast_to(row, (C, C)).T[:, 0:1]

    up.wait_recv()
    down.wait_recv()
    proj = proj_ref[...].astype(F32)
    proj = jnp.concatenate([proj] * slots, axis=0).astype(BF)
    s0 = (dot(proj, xe[0:48, :], TN) + bias).astype(BF).astype(F32)
    fill_taps(t0, s0 * logistic(s0), D1, g)

    w1 = (rays + 2 * D2) * g
    s1 = s0[:, D1 * g : D1 * g + w1] + conv(k1_ref, t0, 0, D1 * g, w1)
    s1 = s1.astype(BF).astype(F32)
    fill_taps(t1, s1 * logistic(s1), D2, g)
    s2 = s1[:, D2 * g : D2 * g + n] + conv(k2_ref, t1, 0, D2 * g, n)
    s2 = s2.astype(BF)

    jb = dot(head_ref[...], xe[48:60, :], TN).astype(BF)
    join = dot(s2, jb[:, HALO * g : HALO * g + n], NT) * scale
    share, own, chunk = parts[0]
    for k in range(naz):
        packs[0][k * chunk + share : (k + 1) * chunk, :] = join[k * own : (k + 1) * own, :]

    g2 = dot(wj_ref[...], jb, NN)
    fill_taps(tu2, g2, D2, g)
    for p in range(3):
        part = dot(
            t1[:, p * D2 * g : p * D2 * g + n], tu2[C : 2 * C, HALO * g : HALO * g + n], NT
        )
        put(0, p * 3 * C, part * scale)
    a0 = phase_a(0)

    joined = dot(wj_ref[...], s2, TN).astype(BF)
    pbuf[e] = dot(head_ref[...], joined, NN)

    wb = (rays + 2 * D1) * g
    g1 = g2[:, D2 * g : D2 * g + wb] + back(k2_ref, tu2, D2 * g, wb) * slope(
        s1[:, (D2 - D1) * g : (D2 - D1) * g + wb]
    )
    b0 = phase_b(0, a0)
    fill_taps(tu1, g1, D1, g)
    for p in range(3):
        first = (HALO + D1 * (p - 1)) * g
        part = dot(t0[:, first : first + n], tu1[C : 2 * C, D1 * g : D1 * g + n], NT)
        put(1, p * 3 * C, part * scale)
    g0 = g1[:, D1 * g : D1 * g + n] + back(k1_ref, tu1, D1 * g, n) * slope(
        s0[:, HALO * g : HALO * g + n]
    )
    g0 = g0.astype(BF)
    gin = dot(xe[0:48, HALO * g : HALO * g + n], g0, NT)
    put(1, 9 * C, (gin[0:24, :] + gin[24:48, :]) * scale)
    summed = dot(jnp.ones((8, n), BF), g0, NT)[0:1, :] * scale
    lines = up8(sweeps)
    index = lax.broadcasted_iota(jnp.int32, (lines, C), 0)
    grads = jnp.zeros((lines, C), F32)
    for s in range(sweeps):
        grads = grads + jnp.where(index == s, owns[s] * summed, 0.0)
    put(1, 9 * C + 24, grads)
    a1 = phase_a(1)
    acc0, c0 = phase_c(0, b0)
    b1 = phase_b(1, a1)
    d0 = phase_d(0, acc0, c0)
    preds = [
        send(pbuf.at[e], pbuf.at[e], sp.at[t], rp.at[t], column[t]) for t in range(1, nel)
    ]
    acc1, c1 = phase_c(1, b1)
    d1 = phase_d(1, acc1, c1)
    e0 = phase_e(0, d0)
    for c in preds:
        c.wait_recv()
    pred = pbuf[0]
    for t in range(1, nel):
        pred = pred + pbuf[t]
    pred_out[...] = pred
    for c in e0:
        c.wait_recv()
    take(0, second_out, 0)
    for k in range(naz):
        join_out[k * own : (k + 1) * own, :] = gbufs[0][
            k * chunk + share : (k + 1) * chunk, :
        ].astype(F32)
    e1 = phase_e(1, d1)
    for c in e1:
        c.wait_recv()
    take(1, first_out, 0)
    take(1, input_out, 9 * C)
    take(1, embed_out, 9 * C + 24)
    for c in started:
        c.wait_send()


def write_kernel(*refs):
    ins, outs, (lines, sems) = refs[0:6], refs[6:12], refs[12:14]
    copies = [pltpu.make_async_copy(ins[i], outs[i], sems.at[i]) for i in range(1, 6)]
    for c in copies:
        c.start()
    leads, n = ins[0].shape
    tiles = n // C
    for t in range(tiles):
        lines[pl.ds(t, leads, stride=tiles), :] = ins[0][:, t * C : (t + 1) * C]
    last = pltpu.make_async_copy(lines, outs[0], sems.at[0])
    last.start()
    for c in copies:
        c.wait()
    last.wait()


def shards(
    raw_sweeps, sweep_ids, elevation_embed, input_proj, first_kernel, second_kernel,
    join_weight, head_weight, cotangent,
):
    naz = lax.axis_size("az")
    nel = lax.axis_size("el")
    slots, _, inputs, rays, gates = raw_sweeps.shape
    leads = head_weight.shape[0]
    sweeps = elevation_embed.shape[0]
    parts = layouts(sweeps, naz)
    scale = 1.0 / math.sqrt(nel * rays * naz * gates)
    n = rays * gates
    h = HALO * gates
    nq = naz // 2

    xc = jnp.concatenate(
        [
            raw_sweeps.reshape(slots * inputs, n),
            cotangent.reshape(leads, n),
        ],
        axis=0,
    )
    vm = pl.BlockSpec(memory_space=pltpu.VMEM)
    dma = pltpu.SemaphoreType.DMA

    def both(shape, kind=BF):
        return [pltpu.VMEM(shape(chunk), kind) for _, _, chunk in parts]

    pred, join, first, second, gin, emb = pl.pallas_call(
        functools.partial(step_kernel, parts, naz, nel, gates, rays, scale),
        out_shape=(
            jax.ShapeDtypeStruct((leads, n), F32),
            jax.ShapeDtypeStruct((C, C), F32),
            jax.ShapeDtypeStruct((9 * C, C), F32),
            jax.ShapeDtypeStruct((9 * C, C), F32),
            jax.ShapeDtypeStruct((inputs, C), F32),
            jax.ShapeDtypeStruct((sweeps, C), F32),
        ),
        in_specs=[pl.BlockSpec(memory_space=pltpu.SMEM)] + [vm] * 7,
        out_specs=(vm,) * 6,
        scratch_shapes=[
            pltpu.VMEM((60, n + 2 * h), BF),
            pltpu.VMEM((3 * C, n + 2 * h), BF),
            pltpu.VMEM((3 * C, (rays + 2 * D2) * gates), BF),
            pltpu.VMEM((3 * C, n + 2 * h), BF),
            pltpu.VMEM((3 * C, (rays + 2 * D1) * gates), BF),
        ]
        + both(lambda chunk: (naz * chunk, C), F32)
        + both(lambda chunk: (naz * chunk, C))
        + both(lambda chunk: (nq * chunk, C))
        + both(lambda chunk: (nq * chunk, C))
        + both(lambda chunk: (nq, chunk, C))
        + both(lambda chunk: (nel, chunk, C))
        + both(lambda chunk: (naz * chunk, C))
        + [
            pltpu.VMEM((nel, leads, n), F32),
            dma((2,)), dma((2,)),
            dma((2,)), dma((2,)),
            dma((2, nq)), dma((2, nq)),
            dma((2, nel)), dma((2, nel)),
            dma((2, nq)), dma((2, nq)),
            dma((2, nq)), dma((2, nq)),
            dma((nel,)), dma((nel,)),
        ],
        compiler_params=pltpu.CompilerParams(
            collective_id=0, has_side_effects=True, vmem_limit_bytes=48 * 1024 * 1024
        ),
        name="step",
    )(
        sweep_ids, xc, elevation_embed, input_proj,
        first_kernel.reshape(9 * C, C), second_kernel.reshape(9 * C, C),
        join_weight[0], head_weight,
    )
    tiles = n // C
    arrays = (pred, join, first, second, gin, emb)
    kinds = [jax.ShapeDtypeStruct((leads * tiles, C), F32)]
    kinds += [jax.ShapeDtypeStruct(v.shape, F32) for v in arrays[1:]]
    pred, join, first, second, gin, emb = pl.pallas_call(
        write_kernel,
        out_shape=tuple(kinds),
        in_specs=[vm] * 6,
        out_specs=(pl.BlockSpec(memory_space=pl.ANY),) * 6,
        scratch_shapes=[pltpu.VMEM((leads * tiles, C), F32), dma((6,))],
        compiler_params=pltpu.CompilerParams(vmem_limit_bytes=4 * 1024 * 1024),
        name="write",
    )(*arrays)
    shape = first_kernel.shape
    return (
        pred.reshape(1, leads, rays, gates),
        join[None],
        first.reshape(shape),
        second.reshape(shape),
        gin,
        emb,
    )


def solution(mesh):
    in_specs = (
        P("el", None, None, "az", None),
        P("el"),
        P(),
        P(),
        P(),
        P(),
        P("el", None, None),
        P(),
        P(None, None, "az", None),
    )
    out_specs = (P(None, None, "az", None), P("el", None, None), P(), P(), P(), P())
    return jax.shard_map(shards, mesh=mesh, in_specs=in_specs, out_specs=out_specs, check_vma=False)
```
